32 devices in a mesh: groups: 2 (over x), row: 4 (over y, core), col: 4 (over z).
Axes of the slice: x: 2, y: 2, z: 4, core: 2. Of those that a mesh axis runs over, the one named last changes fastest.
Arguments:
- observed: float32 [2048, 2048], P(('groups', 'row'), 'col'), parts along dimension 0, may hold values from -24 to 24
- estimate: float32 [2048, 2048], P(('groups', 'row'), 'col'), parts along dimension 0, may hold values from -6 to 6
- kernel: float32 [512, 256], P(('groups', 'row')), parts along dimension 0, may hold values from -6 to 6
Outputs:
- refined: float32 [2048, 2048], P(('groups', 'row'), 'col'), parts along dimension 0
- new_kernel: float32 [512, 256], P(('groups', 'row')), parts along dimension 0
The draws below stay inside these ranges and needn't reach their ends.
There are 2 independent parts, one for each index of `groups`. The reference program is written for one: setup_inputs(seed, part) draws one part's arguments, and reference() takes and returns one part's arrays. A program takes and returns all parts, laid end to end along the dimension named above; each array names one. Nothing has to cross between parts.
All inputs are finite; a program needn't handle non-finite values.
Results may differ from the reference program's by a relative error of at most 0.0001.
Values sent between devices are 32-bit elements; how exact they have to be, the bound alone decides.
A program may use at most 128 MiB of HBM per device.

```python
import jax
import jax.numpy as jnp

K = 256
ITERS = 1
NR = 1024
NC = 2048


def draw_observed(key, part):
    rows_frac = jnp.arange(NR, dtype=jnp.float32)[:, None] / (NR - 1)
    cols_frac = jnp.arange(NC, dtype=jnp.float32)[None, :] / (NC - 1)
    ramped = 10.0 ** (0.5 * rows_frac + 0.5 * cols_frac)
    values = jnp.clip(jax.random.normal(key, (NR, NC), jnp.float32), -6.0, 6.0)
    return (values * ramped * 0.4).astype(jnp.float32)


def block_scale(stream_key, shape, cuts, low, top_value):
    gain = 1.0
    for axis_at, blocks in cuts:
        steps = jax.random.uniform(jax.random.fold_in(jax.random.fold_in(stream_key, 6), axis_at), (blocks,), jnp.float32, low / len(cuts), top_value / len(cuts))
        gain = gain * jnp.repeat(jnp.exp(steps), shape[axis_at] // blocks).reshape((-1,) + (1,) * (len(shape) - 1 - axis_at))
    return gain


def gaussian(own_key, extent, deviation, reach, pieces=(), held_as=jnp.bfloat16):
    gain = block_scale(own_key, extent, pieces, -0.22, 0.18) if pieces else 1.0
    entries = jax.random.normal(own_key, extent, jnp.float32) * deviation * gain
    return jnp.minimum(jnp.maximum(entries, -reach), reach).astype(held_as)


def setup_inputs(seed: int = 0, part: int = 0) -> dict:
    splits = jax.random.split(jax.random.key(seed), 4)
    part_keys = jax.random.split(jax.random.fold_in(splits[3], part), 4)
    return {
        "observed": draw_observed(jax.random.fold_in(jax.random.fold_in(splits[3], part), 71), part),
        "estimate": gaussian(part_keys[1], (NR, NC), 1.0, 6.0, ((0, 4), (1, 4)), jnp.float32),
        "kernel": gaussian(part_keys[2], (K, K), 1.0, 6.0, ((0, 4),), jnp.float32),
    }


EPSILON = 1e-6


def reference(observed, estimate, kernel):
    half = K // 2
    long_rows = NR + K
    long_cols = NC + K
    factor = 1.0 / K

    def spectrum(field):
        return jnp.fft.rfft2(field, s=(long_rows, long_cols))

    def spatial(spec):
        return jnp.fft.irfft2(spec, s=(long_rows, long_cols))

    image = estimate
    psf = kernel
    for sweep in range(ITERS):
        placed = jnp.pad(psf, ((0, long_rows - K), (0, long_cols - K)))
        placed = jnp.roll(placed, (-half, -half), axis=(0, 1))
        transfer = spectrum(placed)
        image_spec = spectrum(image)
        predicted = spatial(image_spec * transfer)[:NR, :NC] * factor
        residual = predicted - observed
        residual_spec = spectrum(residual)
        image_grad = spatial(residual_spec * jnp.conj(transfer))[:NR, :NC] * factor
        lagged = jnp.roll(spatial(residual_spec * jnp.conj(image_spec)), (half, half), axis=(0, 1))
        psf_grad = lagged[:K, :K] * factor
        loss = 0.5 * jnp.sum(residual * residual)
        image_norm = jnp.sum(image_grad * image_grad)
        psf_norm = jnp.sum(psf_grad * psf_grad)
        image = image - (loss / (image_norm + EPSILON)) * image_grad
        psf = psf - (0.25 * loss / (psf_norm + EPSILON)) * psf_grad
    return image.astype(jnp.float32), psf.astype(jnp.float32)
```

```python
import functools
import math

import jax
import jax.numpy as jnp
import numpy as np
from jax import lax
from jax.experimental import pallas as pl
from jax.experimental.pallas import tpu as pltpu
from jax.sharding import PartitionSpec as P

EPSILON = 1e-06
MESH = pl.DeviceIdType.MESH
FEW = 16
VMEM = pltpu.VMEM
BF16 = jnp.bfloat16
F32 = jnp.float32
ROOT = math.sqrt(3.0) / 2.0
AROUND = [(a, b) for a in (-1, 0, 1) for b in (-1, 0, 1) if (a, b) != (0, 0)]


def here(row, col, n_row, n_col):
    return (row >= 0) & (row < n_row) & (col >= 0) & (col < n_col)


def others(n_row, n_col):
    return [(s, t) for s in range(n_row) for t in range(n_col) if (s, t) != (0, 0)]


def peer(row, col, s, t, n_row, n_col):
    return {"row": lax.rem(row + s, n_row), "col": lax.rem(col + t, n_col)}


def spans(tile, margin):
    inner = {-1: (0, margin), 0: (0, tile), 1: (tile - margin, margin)}
    outer = {-1: (tile + margin, margin), 0: (0, tile), 1: (tile, margin)}
    return inner, outer


def at(ref, rows, cols):
    return ref.at[pl.ds(*rows), pl.ds(*cols)]


def line(x):
    rows, cols = x.shape
    if rows % 8:
        x = jnp.concatenate([x, jnp.zeros((8 - rows % 8, cols), F32)], axis=0)
        rows = x.shape[0]
    x = (x * x).reshape(rows // 8, 8, cols).sum(axis=0)
    total = x[:, :128]
    for at_col in range(128, cols, 128):
        total = total + x[:, at_col : at_col + 128]
    return jnp.sum(total, axis=0, keepdims=True)


def halves(x):
    high = x.astype(BF16)
    return high, (x - high.astype(F32)).astype(BF16)


def dot3(a, b):
    dot = lambda p, q: lax.dot_general(p, q, (((1,), (0,)), ((), ())), preferred_element_type=F32)
    return dot(a[0], b[0]) + (dot(a[0], b[1]) + dot(a[1], b[0]))


def body(
    n_row, n_col, observed, estimate, kernel, *rest
):
    tables, rest = rest[:11], rest[11:]
    refined, new_kernel = rest[:2]
    held, rest = rest[2:13], rest[13:]
    (wide, wider, obs, own, full, near_t, spec_i, spec_k, spec_r, mixed, kgrad, pland,
     cpart, cland, pieces, srow, scol, sums, *sems) = rest
    (ls, hs, hr, ks, kr, bs, br, ps, cs, cr, gs, gr, as_, ar, es, er) = sems
    (lag_fwd, lag_inv, own_fwd, own_fwd1, side_fwd, own_inv, own_inv1,
     row_lag, row_own, inv_own, inv_lag) = held
    row, col = lax.axis_index("row"), lax.axis_index("col")
    tile_rows, tile_cols = observed.shape
    owner, side = kernel.shape
    margin = side // 2
    rows_long, cols_long = tile_rows + side, tile_cols + side
    in_r, out_r = spans(tile_rows, margin)
    in_c, out_c = spans(tile_cols, margin)
    pairs = n_row // 2
    core = lax.rem(row, 2)
    twin = row + 1 - 2 * core
    few = owner // n_col

    def copy(src, dst, ssem, rsem, **target):
        return pltpu.make_async_remote_copy(
            src_ref=src, dst_ref=dst, send_sem=ssem, recv_sem=rsem,
            device_id=target, device_id_type=MESH,
        )

    def halo(i, src, dst, ssem, rsem):
        dr, dc = AROUND[i]
        return copy(
            at(src, in_r[dr], in_c[dc]), at(dst, out_r[-dr], out_c[-dc]),
            ssem.at[i], rsem.at[i], row=row + dr, col=col + dc,
        )

    def target_of(i):
        dr, dc = AROUND[i]
        return here(row + dr, col + dc, n_row, n_col)

    def source_of(i):
        dr, dc = AROUND[i]
        return here(row - dr, col - dc, n_row, n_col)

    def block(r):
        return pl.ds(pl.multiple_of(r * owner, owner), owner)

    barrier = pltpu.get_barrier_semaphore()
    for s, t in others(n_row, n_col):
        pl.semaphore_signal(
            barrier, inc=1, device_id=peer(row, col, s, t, n_row, n_col), device_id_type=MESH
        )
    near, far = slice(0, tile_rows), slice(tile_rows, rows_long)
    loads = [
        pltpu.make_async_copy(estimate, wide.at[near, :tile_cols], ls.at[0]),
        pltpu.make_async_copy(kernel, own, ls.at[1]),
        pltpu.make_async_copy(observed, obs, ls.at[2]),
    ]
    order = (2, 3, 0, 7, 4, 8, 9, 5, 6, 10, 1)
    fetch = {
        k: pltpu.make_async_copy(tables[k], held[k], ls.at[3 + k]) for k in order
    }
    for one in loads:
        one.start()
    for k in order:
        fetch[k].start()
    pl.semaphore_wait(barrier, n_row * n_col - 1)

    def gather(k):
        if k == 0:
            return copy(kernel, full.at[block(row), :], ks.at[0], kr.at[0], row=twin)
        if k < pairs:
            there = lax.rem(row + 2 * k, n_row)
            return copy(kernel, full.at[block(row), :], ks.at[k], kr.at[k], row=there)
        behind = lax.rem(row + n_row - 2 * (k - pairs + 1), n_row)
        return copy(
            full.at[block(behind), :], full.at[block(behind), :], ks.at[k], kr.at[k], row=twin
        )

    for k in range(pairs):
        gather(k).start()
    for i in range(8):

        @pl.when(target_of(i))
        def _():
            halo(i, estimate, wide, hs, hr).start()

    for i, (dr, dc) in enumerate(AROUND):

        @pl.when(jnp.logical_not(source_of(i)))
        def _():
            empty = jnp.zeros((out_r[-dr][1], out_c[-dc][1]), F32)
            wide[pl.ds(*out_r[-dr]), pl.ds(*out_c[-dc])] = empty
            wider[pl.ds(*out_r[-dr]), pl.ds(*out_c[-dc])] = empty

    def pair(ref, rows=slice(None), cols=slice(None)):
        return ref[0, rows, cols], ref[1, rows, cols]

    def three(x):
        return x[:, :side], x[:, side : 2 * side]

    def columns(x0, x1, x2=None):
        if x2 is None:
            u, v, w = x0 + 0.5 * x1, -ROOT * x1, x0 - x1
        else:
            u, v, w = x0 + 0.5 * (x1 - x2), -ROOT * (x1 + x2), x0 - x1 + x2
        return (
            dot3(halves(jnp.concatenate([u, v], axis=1)), pair(own_fwd)),
            dot3(halves(w), pair(own_fwd1)),
        )

    parts = (
        (slice(0, side), slice(side, 2 * side)),
        (slice(2 * side, 2 * side + margin), slice(2 * side + margin, 3 * side)),
    )

    def unfold(spec, base, out):
        step = 32
        for k in range(margin // step):
            here_ = slice(k * step, (k + 1) * step)
            there = slice(margin + k * step, margin + (k + 1) * step)
            up = slice(base + k * step, base + (k + 1) * step)
            down = slice(base + margin + k * step, base + margin + (k + 1) * step)
            for re, im in parts:
                pr, pi, qr, qi = out[here_, re], out[here_, im], out[there, re], out[there, im]
                ur, ui, dr, di = pr + qi, pi - qr, pr - qi, pi + qr
                if base == 0 and k == 0:
                    first = lax.broadcasted_iota(jnp.int32, ur.shape, 0) == 0
                    ur, ui = jnp.where(first, pr, ur), jnp.where(first, pi, ui)
                    dr, di = jnp.where(first, qr, dr), jnp.where(first, qi, di)
                spec[up, re], spec[up, im] = ur, ui
                spec[down, re], spec[down, im] = dr, di

    def multiply(a, b, conj):
        step = 16
        for base in (0, side):
            for k in range(margin // step):
                up = slice(base + k * step, base + (k + 1) * step)
                down = slice(base + margin + k * step, base + margin + (k + 1) * step)
                for re, im in parts:
                    both = []
                    for rows in (up, down):
                        xr, xi, yr, yi = a[rows, re], a[rows, im], b[rows, re], b[rows, im]
                        if conj:
                            both.append((xr * yr + xi * yi, xi * yr - xr * yi))
                        else:
                            both.append((xr * yr - xi * yi, xr * yi + xi * yr))
                    (ur, ui), (dr, di) = both
                    cr_, ci_, sr_, si_ = ur + dr, ui + di, di - ui, ur - dr
                    if base == 0 and k == 0:
                        first = lax.broadcasted_iota(jnp.int32, ur.shape, 0) == 0
                        cr_, ci_ = jnp.where(first, ur, cr_), jnp.where(first, ui, ci_)
                        sr_, si_ = jnp.where(first, dr, sr_), jnp.where(first, di, si_)
                    for rows, cols, v in ((up, re, cr_), (up, im, ci_), (down, re, sr_), (down, im, si_)):
                        high, low = halves(v)
                        mixed[0, rows, cols] = high
                        mixed[1, rows, cols] = low

    def rows_forward(spec, table, x):
        for base in (0, side):
            unfold(spec, base, dot3(pair(table, slice(base, base + side)), x))

    def own_columns(ref):
        s0, s1 = columns(*three(ref[near, :tile_cols]))
        near_t[:, : 2 * side] = s0
        near_t[:, 2 * side :] = s1

    def spectrum_of(ref, spec):
        beside = near_t[...] + dot3(halves(ref[near, tile_cols:]), pair(side_fwd))
        x0, x1 = three(ref[far, :tile_cols])
        x2 = jnp.concatenate(
            [ref[far, tile_cols : tile_cols + margin], -ref[far, tile_cols + margin :]], axis=1
        )
        below = jnp.concatenate(columns(x0, x1, x2), axis=1)
        unfold(spec, 0, dot3(pair(row_own, slice(0, side)), halves(beside + below)))
        unfold(spec, side, dot3(pair(row_own, slice(side, 2 * side)), halves(beside - below)))

    def own_values():
        high, low = halves(dot3(pair(inv_own), pair(mixed)))
        head, tail = slice(0, 2 * side), slice(2 * side, 3 * side)
        v = dot3((high[:, head], low[:, head]), pair(own_inv))
        w = dot3((high[:, tail], low[:, tail]), pair(own_inv1))
        vr, vi = v[:, :side], v[:, side:]
        return vr + w, 0.5 * vr - ROOT * vi - w

    loads[0].wait()
    fetch[2].wait()
    fetch[3].wait()
    own_columns(wide)

    loads[1].wait()
    full[block(row), :] = own[...]
    for k in range(1, pairs):
        gather(k).wait_recv()
        gather(k + pairs - 1).start()
    gather(0).wait_recv()
    for k in range(pairs, 2 * pairs - 1):
        gather(k).wait_recv()
    fetch[0].wait()
    fetch[7].wait()
    rows_forward(spec_k, row_lag, halves(dot3(halves(full[...]), pair(lag_fwd))))

    for k in (1, 4, 5, 6, 8, 9, 10):
        fetch[k].wait()
    loads[2].wait()
    for i in range(8):

        @pl.when(source_of(i))
        def _():
            halo(i, estimate, wide, hs, hr).wait_recv()

    spectrum_of(wide, spec_i)
    multiply(spec_i, spec_k, False)
    x0, x1 = own_values()
    x0, x1 = x0 - obs[:, :side], x1 - obs[:, side:]
    wider[near, :side] = x0
    wider[near, side:tile_cols] = x1
    for i in range(8):

        @pl.when(target_of(i))
        def _():
            halo(i, wider, wider, bs, br).start()

    sums[...] = jnp.zeros_like(sums)
    sums[0:1] = line(x0) + line(x1)
    own_columns(wider)
    rows_forward(spec_r, row_own, halves(near_t[...]))
    multiply(spec_r, spec_i, True)
    kgrad[...] = dot3(halves(dot3(pair(inv_lag), pair(mixed))), pair(lag_inv))

    def share(c):
        return pl.ds(pl.multiple_of(c * margin, margin), margin)

    swap = copy(kgrad.at[share(1 - core), :], pland, ps.at[0], ps.at[1], row=twin)
    swap.start()
    swap.wait()
    mine = kgrad[share(core), :] + pland[...]
    for k in range(pairs * n_col):
        cpart[k] = mine[k * few : (k + 1) * few]
    half_row = row // 2
    scatter = []
    for s, t in others(pairs, n_col):
        r, c = lax.rem(half_row + s, pairs), lax.rem(col + t, n_col)
        k = s * n_col + t - 1
        scatter.append(copy(
            cpart.at[r * n_col + c], cland.at[k], cs.at[k], cr.at[k], row=2 * r + core, col=c
        ))
    for one in scatter:
        one.start()

    for i in range(8):

        @pl.when(source_of(i))
        def _():
            halo(i, wider, wider, bs, br).wait_recv()

    spectrum_of(wider, spec_r)
    multiply(spec_r, spec_k, True)
    x0, x1 = own_values()
    refined[:, :side] = x0
    refined[:, side:] = x1
    sums[1:2] = line(x0) + line(x1)

    piece = cpart[half_row * n_col + col]
    for k, one in enumerate(scatter):
        one.wait()
        piece = piece + cland[k]
    pieces[col] = piece
    sums[2:3] = line(piece)
    gathers = [
        copy(pieces.at[col], pieces.at[col], gs.at[s - 1], gr.at[s - 1], col=lax.rem(col + s, n_col))
        for s in range(1, n_col)
    ]

    def total_of(buf):
        added = buf[0]
        for k in range(1, buf.shape[0]):
            added = added + buf[k]
        return added

    if n_row * n_col <= FEW:
        me = row * n_col + col
        srow[me] = sums[...]
        parts_ = [
            copy(srow.at[me], srow.at[me], as_.at[k], ar.at[k], **peer(row, col, s, t, n_row, n_col))
            for k, (s, t) in enumerate(others(n_row, n_col))
        ]
        for one in parts_ + gathers:
            one.start()
        for one in parts_:
            one.wait()
        added = total_of(srow)
    else:
        srow[row] = sums[...]
        parts_ = [
            copy(srow.at[row], srow.at[row], as_.at[s - 1], ar.at[s - 1], row=lax.rem(row + s, n_row))
            for s in range(1, n_row)
        ]
        for one in parts_ + gathers:
            one.start()
        for one in parts_:
            one.wait()
        scol[col] = total_of(srow)
        parts_ = [
            copy(scol.at[col], scol.at[col], es.at[s - 1], er.at[s - 1], col=lax.rem(col + s, n_col))
            for s in range(1, n_col)
        ]
        for one in parts_:
            one.start()
        for one in parts_:
            one.wait()
        added = total_of(scol)
    loss = 0.5 * jnp.sum(added[0:1], keepdims=True)
    image_norm = jnp.sum(added[1:2], keepdims=True)
    kernel_norm = jnp.sum(added[2:3], keepdims=True)
    refined[...] = wide[near, :tile_cols] - refined[...] * (loss / (image_norm + EPSILON))
    rate = 0.25 * loss / (kernel_norm + EPSILON)
    for one in gathers:
        one.wait()
    for c in range(n_col):
        rows = slice(c * few, (c + 1) * few)
        new_kernel[rows, :] = own[rows, :] - pieces[c] * rate
    for k in range(2 * pairs - 1):
        gather(k).wait_send()
    for i in range(8):

        @pl.when(target_of(i))
        def _():
            halo(i, estimate, wide, hs, hr).wait_send()
            halo(i, wider, wider, bs, br).wait_send()


def split(x):
    high = np.asarray(x, np.float32).astype(jnp.bfloat16)
    low = (np.asarray(x, np.float32) - high.astype(np.float32)).astype(jnp.bfloat16)
    return jnp.asarray(np.stack([high, low]))


def make_tables(n_row, owner, side):
    margin = side // 2
    wide, tall = 3 * side, 2 * side
    scale = 2.0 / (wide * tall) / side
    inside, centred = np.arange(side), np.arange(side) - margin

    def waves(places, freqs, period):
        phase = np.mod(np.outer(places, freqs), period) * (2 * math.pi / period)
        return np.cos(phase), np.sin(phase)

    first, second = 6 * np.arange(side) + 1, 6 * np.arange(margin) + 3

    def line_table(places):
        c0, s0 = waves(places, first, 2 * wide)
        c1, s1 = waves(places, second, 2 * wide)
        return np.concatenate([c0, -s0, c1, -s1], axis=1)

    c0, s0 = waves(inside, first, 2 * wide)
    c1, s1 = waves(inside, second, 2 * wide)
    own_fwd = np.block([[c0, -s0], [s0, c0]])
    own_fwd1 = np.concatenate([c1, -s1], axis=1)
    beside = np.concatenate([2 * side + np.arange(margin), np.arange(margin) - margin])

    def row_table(places):
        j = np.arange(margin)
        ce, se = waves(2 * j, places, tall)
        se[0] = np.cos(math.pi * places)
        co, so = waves(2 * j + 1, places, tall)
        return np.concatenate([ce, se, co, so], axis=0)

    blocks = list(range(0, n_row, 2)) + list(range(1, n_row, 2))
    turned = np.concatenate([np.arange(r * owner, (r + 1) * owner) for r in blocks])
    lag = line_table(centred)
    return [
        split(x)
        for x in (
            lag, lag.T * scale, own_fwd, own_fwd1, line_table(beside), own_fwd.T * scale,
            own_fwd1.T * scale, row_table(centred), row_table(inside), row_table(inside).T,
            row_table(centred).T[turned],
        )
    ]


def per_device(n_row, n_col, observed, estimate, kernel):
    tile_rows, tile_cols = observed.shape
    owner, side = kernel.shape
    margin = side // 2
    rows_long, cols_long = tile_rows + side, tile_cols + side
    tables = make_tables(n_row, owner, side)
    dma = pltpu.SemaphoreType.DMA
    more_c = max(n_col - 1, 1)
    few = owner // n_col
    pairs = n_row // 2
    firsts = n_row * n_col if n_row * n_col <= FEW else n_row
    spectrum = VMEM((rows_long, cols_long), F32)
    more_p = max(pairs * n_col - 1, 1)
    return pl.pallas_call(
        functools.partial(body, n_row, n_col),
        out_shape=(
            jax.ShapeDtypeStruct((tile_rows, tile_cols), F32),
            jax.ShapeDtypeStruct((owner, side), F32),
        ),
        in_specs=[pl.BlockSpec(memory_space=pl.ANY)] * (3 + len(tables)),
        out_specs=(pl.BlockSpec(memory_space=VMEM),) * 2,
        scratch_shapes=[VMEM(x.shape, BF16) for x in tables] + [
            spectrum,
            spectrum,
            VMEM((tile_rows, tile_cols), F32),
            VMEM((owner, side), F32),
            VMEM((side, side), F32),
            VMEM((tile_rows, cols_long), F32),
            spectrum,
            spectrum,
            spectrum,
            VMEM((2, rows_long, cols_long), BF16),
            VMEM((side, side), F32),
            VMEM((margin, side), F32),
            VMEM((pairs * n_col, few, side), F32),
            VMEM((more_p, few, side), F32),
            VMEM((n_col, few, side), F32),
            VMEM((firsts, 8, 128), F32),
            VMEM((n_col, 8, 128), F32),
            VMEM((8, 128), F32),
            dma((3 + len(tables),)),
            dma((8,)), dma((8,)),
            dma((n_row,)), dma((n_row,)),
            dma((8,)), dma((8,)),
            dma((2,)),
            dma((more_p,)), dma((more_p,)),
            dma((more_c,)), dma((more_c,)),
            dma((firsts,)), dma((firsts,)),
            dma((more_c,)), dma((more_c,)),
        ],
        compiler_params=pltpu.CompilerParams(
            collective_id=0, has_side_effects=True, vmem_limit_bytes=63 * 1024 * 1024
        ),
        name="deconvolve",
    )(observed, estimate, kernel, *tables)


def solution(mesh):
    placed = (P(("groups", "row"), "col"), P(("groups", "row"), "col"), P(("groups", "row"), None))
    return jax.shard_map(
        functools.partial(per_device, mesh.shape["row"], mesh.shape["col"]),
        mesh=mesh,
        in_specs=placed,
        out_specs=(P(("groups", "row"), "col"), P(("groups", "row"), None)),
        check_vma=False,
    )
```

```python
import functools
import math

import jax
import jax.numpy as jnp
import numpy as np
from jax import lax
from jax.experimental import pallas as pl
from jax.experimental.pallas import tpu as pltpu
from jax.sharding import PartitionSpec as P

EPSILON = 1e-06
MESH = pl.DeviceIdType.MESH
FEW = 16
VMEM = pltpu.VMEM
BF16 = jnp.bfloat16
F32 = jnp.float32
ROOT = math.sqrt(3.0) / 2.0
AROUND = [(a, b) for a in (-1, 0, 1) for b in (-1, 0, 1) if (a, b) != (0, 0)]


def here(row, col, n_row, n_col):
    return (row >= 0) & (row < n_row) & (col >= 0) & (col < n_col)


def others(n_row, n_col):
    return [(s, t) for s in range(n_row) for t in range(n_col) if (s, t) != (0, 0)]


def peer(row, col, s, t, n_row, n_col):
    return {"row": lax.rem(row + s, n_row), "col": lax.rem(col + t, n_col)}


def spans(tile, margin):
    inner = {-1: (0, margin), 0: (0, tile), 1: (tile - margin, margin)}
    outer = {-1: (tile + margin, margin), 0: (0, tile), 1: (tile, margin)}
    return inner, outer


def at(ref, rows, cols):
    return ref.at[pl.ds(*rows), pl.ds(*cols)]


def line(x):
    rows, cols = x.shape
    if rows % 8:
        x = jnp.concatenate([x, jnp.zeros((8 - rows % 8, cols), F32)], axis=0)
        rows = x.shape[0]
    x = (x * x).reshape(rows // 8, 8, cols).sum(axis=0)
    total = x[:, :128]
    for at_col in range(128, cols, 128):
        total = total + x[:, at_col : at_col + 128]
    return jnp.sum(total, axis=0, keepdims=True)


def halves(x):
    high = x.astype(BF16)
    return high, (x - high.astype(F32)).astype(BF16)


def dot3(a, b):
    dot = lambda p, q: lax.dot_general(p, q, (((1,), (0,)), ((), ())), preferred_element_type=F32)
    return dot(a[0], b[0]) + (dot(a[0], b[1]) + dot(a[1], b[0]))


def body(
    n_row, n_col, observed, estimate, kernel, *rest
):
    tables, rest = rest[:11], rest[11:]
    refined, new_kernel = rest[:2]
    held, rest = rest[2:13], rest[13:]
    (wide, wider, obs, own, full, near_t, spec_i, spec_k, spec_r, mixed, kgrad, pland,
     cpart, cland, pieces, srow, scol, sums, *sems) = rest
    (ls, hs, hr, ks, kr, bs, br, ps, cs, cr, gs, gr, as_, ar, es, er) = sems
    (lag_fwd, lag_inv, own_fwd, own_fwd1, side_fwd, own_inv, own_inv1,
     row_lag, row_own, inv_own, inv_lag) = held
    row, col = lax.axis_index("row"), lax.axis_index("col")
    tile_rows, tile_cols = observed.shape
    owner, side = kernel.shape
    margin = side // 2
    rows_long, cols_long = tile_rows + side, tile_cols + side
    in_r, out_r = spans(tile_rows, margin)
    in_c, out_c = spans(tile_cols, margin)
    pairs = n_row // 2
    core = lax.rem(row, 2)
    twin = row + 1 - 2 * core
    few = owner // n_col

    def copy(src, dst, ssem, rsem, **target):
        return pltpu.make_async_remote_copy(
            src_ref=src, dst_ref=dst, send_sem=ssem, recv_sem=rsem,
            device_id=target, device_id_type=MESH,
        )

    def halo(i, src, dst, ssem, rsem):
        dr, dc = AROUND[i]
        return copy(
            at(src, in_r[dr], in_c[dc]), at(dst, out_r[-dr], out_c[-dc]),
            ssem.at[i], rsem.at[i], row=row + dr, col=col + dc,
        )

    def target_of(i):
        dr, dc = AROUND[i]
        return here(row + dr, col + dc, n_row, n_col)

    def source_of(i):
        dr, dc = AROUND[i]
        return here(row - dr, col - dc, n_row, n_col)

    def block(r):
        return pl.ds(pl.multiple_of(r * owner, owner), owner)

    barrier = pltpu.get_barrier_semaphore()
    for s, t in others(n_row, n_col):
        pl.semaphore_signal(
            barrier, inc=1, device_id=peer(row, col, s, t, n_row, n_col), device_id_type=MESH
        )
    near, far = slice(0, tile_rows), slice(tile_rows, rows_long)
    loads = [
        pltpu.make_async_copy(estimate, wide.at[near, :tile_cols], ls.at[0]),
        pltpu.make_async_copy(kernel, own, ls.at[1]),
        pltpu.make_async_copy(observed, obs, ls.at[2]),
    ]
    order = (2, 3, 0, 7, 4, 8, 9, 5, 6, 10, 1)
    fetch = {
        k: pltpu.make_async_copy(tables[k], held[k], ls.at[3 + k]) for k in order
    }
    for one in loads:
        one.start()
    for k in order:
        fetch[k].start()
    pl.semaphore_wait(barrier, n_row * n_col - 1)

    def gather(k):
        if k == 0:
            return copy(kernel, full.at[block(row), :], ks.at[0], kr.at[0], row=twin)
        if k < pairs:
            there = lax.rem(row + 2 * k, n_row)
            return copy(kernel, full.at[block(row), :], ks.at[k], kr.at[k], row=there)
        behind = lax.rem(row + n_row - 2 * (k - pairs + 1), n_row)
        return copy(
            full.at[block(behind), :], full.at[block(behind), :], ks.at[k], kr.at[k], row=twin
        )

    for k in range(pairs):
        gather(k).start()
    for i in range(8):

        @pl.when(target_of(i))
        def _():
            halo(i, estimate, wide, hs, hr).start()

    for i, (dr, dc) in enumerate(AROUND):

        @pl.when(jnp.logical_not(source_of(i)))
        def _():
            empty = jnp.zeros((out_r[-dr][1], out_c[-dc][1]), F32)
            wide[pl.ds(*out_r[-dr]), pl.ds(*out_c[-dc])] = empty
            wider[pl.ds(*out_r[-dr]), pl.ds(*out_c[-dc])] = empty

    def pair(ref, rows=slice(None), cols=slice(None)):
        return ref[0, rows, cols], ref[1, rows, cols]

    def three(x):
        return x[:, :side], x[:, side : 2 * side]

    def columns(x0, x1, x2=None):
        if x2 is None:
            u, v, w = x0 + 0.5 * x1, -ROOT * x1, x0 - x1
        else:
            u, v, w = x0 + 0.5 * (x1 - x2), -ROOT * (x1 + x2), x0 - x1 + x2
        return (
            dot3(halves(jnp.concatenate([u, v], axis=1)), pair(own_fwd)),
            dot3(halves(w), pair(own_fwd1)),
        )

    parts = (
        (slice(0, side), slice(side, 2 * side)),
        (slice(2 * side, 2 * side + margin), slice(2 * side + margin, 3 * side)),
    )

    def unfold(spec, base, out):
        step = 32
        for k in range(margin // step):
            here_ = slice(k * step, (k + 1) * step)
            there = slice(margin + k * step, margin + (k + 1) * step)
            up = slice(base + k * step, base + (k + 1) * step)
            down = slice(base + margin + k * step, base + margin + (k + 1) * step)
            for re, im in parts:
                pr, pi, qr, qi = out[here_, re], out[here_, im], out[there, re], out[there, im]
                ur, ui, dr, di = pr + qi, pi - qr, pr - qi, pi + qr
                if base == 0 and k == 0:
                    first = lax.broadcasted_iota(jnp.int32, ur.shape, 0) == 0
                    ur, ui = jnp.where(first, pr, ur), jnp.where(first, pi, ui)
                    dr, di = jnp.where(first, qr, dr), jnp.where(first, qi, di)
                spec[up, re], spec[up, im] = ur, ui
                spec[down, re], spec[down, im] = dr, di

    def multiply(a, b, conj):
        step = 16
        for base in (0, side):
            for k in range(margin // step):
                up = slice(base + k * step, base + (k + 1) * step)
                down = slice(base + margin + k * step, base + margin + (k + 1) * step)
                for re, im in parts:
                    both = []
                    for rows in (up, down):
                        xr, xi, yr, yi = a[rows, re], a[rows, im], b[rows, re], b[rows, im]
                        if conj:
                            both.append((xr * yr + xi * yi, xi * yr - xr * yi))
                        else:
                            both.append((xr * yr - xi * yi, xr * yi + xi * yr))
                    (ur, ui), (dr, di) = both
                    cr_, ci_, sr_, si_ = ur + dr, ui + di, di - ui, ur - dr
                    if base == 0 and k == 0:
                        first = lax.broadcasted_iota(jnp.int32, ur.shape, 0) == 0
                        cr_, ci_ = jnp.where(first, ur, cr_), jnp.where(first, ui, ci_)
                        sr_, si_ = jnp.where(first, dr, sr_), jnp.where(first, di, si_)
                    for rows, cols, v in ((up, re, cr_), (up, im, ci_), (down, re, sr_), (down, im, si_)):
                        high, low = halves(v)
                        mixed[0, rows, cols] = high
                        mixed[1, rows, cols] = low

    def rows_forward(spec, table, x):
        for base in (0, side):
            unfold(spec, base, dot3(pair(table, slice(base, base + side)), x))

    def own_columns(ref):
        s0, s1 = columns(*three(ref[near, :tile_cols]))
        near_t[:, : 2 * side] = s0
        near_t[:, 2 * side :] = s1

    def spectrum_of(ref, spec):
        beside = near_t[...] + dot3(halves(ref[near, tile_cols:]), pair(side_fwd))
        x0, x1 = three(ref[far, :tile_cols])
        x2 = jnp.concatenate(
            [ref[far, tile_cols : tile_cols + margin], -ref[far, tile_cols + margin :]], axis=1
        )
        below = jnp.concatenate(columns(x0, x1, x2), axis=1)
        unfold(spec, 0, dot3(pair(row_own, slice(0, side)), halves(beside + below)))
        unfold(spec, side, dot3(pair(row_own, slice(side, 2 * side)), halves(beside - below)))

    def own_values():
        high, low = halves(dot3(pair(inv_own), pair(mixed)))
        head, tail = slice(0, 2 * side), slice(2 * side, 3 * side)
        v = dot3((high[:, head], low[:, head]), pair(own_inv))
        w = dot3((high[:, tail], low[:, tail]), pair(own_inv1))
        vr, vi = v[:, :side], v[:, side:]
        return vr + w, 0.5 * vr - ROOT * vi - w

    loads[0].wait()
    fetch[2].wait()
    fetch[3].wait()
    own_columns(wide)

    loads[1].wait()
    full[block(row), :] = own[...]
    for k in range(1, pairs):
        gather(k).wait_recv()
        gather(k + pairs - 1).start()
    gather(0).wait_recv()
    for k in range(pairs, 2 * pairs - 1):
        gather(k).wait_recv()
    fetch[0].wait()
    fetch[7].wait()
    rows_forward(spec_k, row_lag, halves(dot3(halves(full[...]), pair(lag_fwd))))

    for k in (1, 4, 5, 6, 8, 9, 10):
        fetch[k].wait()
    loads[2].wait()
    for i in range(8):

        @pl.when(source_of(i))
        def _():
            halo(i, estimate, wide, hs, hr).wait_recv()

    spectrum_of(wide, spec_i)
    multiply(spec_i, spec_k, False)
    x0, x1 = own_values()
    x0, x1 = x0 - obs[:, :side], x1 - obs[:, side:]
    wider[near, :side] = x0
    wider[near, side:tile_cols] = x1
    for i in range(8):

        @pl.when(target_of(i))
        def _():
            halo(i, wider, wider, bs, br).start()

    sums[...] = jnp.zeros_like(sums)
    sums[0:1] = line(x0) + line(x1)
    own_columns(wider)
    rows_forward(spec_r, row_own, halves(near_t[...]))
    multiply(spec_r, spec_i, True)
    kgrad[...] = dot3(halves(dot3(pair(inv_lag), pair(mixed))), pair(lag_inv))

    def share(c):
        return pl.ds(pl.multiple_of(c * margin, margin), margin)

    swap = copy(kgrad.at[share(1 - core), :], pland, ps.at[0], ps.at[1], row=twin)
    swap.start()
    swap.wait()
    mine = kgrad[share(core), :] + pland[...]
    for k in range(pairs * n_col):
        cpart[k] = mine[k * few : (k + 1) * few]
    half_row = row // 2
    scatter = []
    for s, t in others(pairs, n_col):
        r, c = lax.rem(half_row + s, pairs), lax.rem(col + t, n_col)
        k = s * n_col + t - 1
        scatter.append(copy(
            cpart.at[r * n_col + c], cland.at[k], cs.at[k], cr.at[k], row=2 * r + core, col=c
        ))
    for one in scatter:
        one.start()

    for i in range(8):

        @pl.when(source_of(i))
        def _():
            halo(i, wider, wider, bs, br).wait_recv()

    spectrum_of(wider, spec_r)
    multiply(spec_r, spec_k, True)
    x0, x1 = own_values()
    refined[:, :side] = x0
    refined[:, side:] = x1
    sums[1:2] = line(x0) + line(x1)

    piece = cpart[half_row * n_col + col]
    for k, one in enumerate(scatter):
        one.wait()
        piece = piece + cland[k]
    pieces[col] = piece
    sums[2:3] = line(piece)
    gathers = [
        copy(pieces.at[col], pieces.at[col], gs.at[s - 1], gr.at[s - 1], col=lax.rem(col + s, n_col))
        for s in range(1, n_col)
    ]

    def total_of(buf):
        added = buf[0]
        for k in range(1, buf.shape[0]):
            added = added + buf[k]
        return added

    if n_row * n_col <= FEW:
        me = row * n_col + col
        srow[me] = sums[...]
        parts_ = [
            copy(srow.at[me], srow.at[me], as_.at[k], ar.at[k], **peer(row, col, s, t, n_row, n_col))
            for k, (s, t) in enumerate(others(n_row, n_col))
        ]
        for one in parts_ + gathers:
            one.start()
        for one in parts_:
            one.wait()
        added = total_of(srow)
    else:
        srow[row] = sums[...]
        parts_ = [
            copy(srow.at[row], srow.at[row], as_.at[s - 1], ar.at[s - 1], row=lax.rem(row + s, n_row))
            for s in range(1, n_row)
        ]
        for one in parts_ + gathers:
            one.start()
        for one in parts_:
            one.wait()
        scol[col] = total_of(srow)
        parts_ = [
            copy(scol.at[col], scol.at[col], es.at[s - 1], er.at[s - 1], col=lax.rem(col + s, n_col))
            for s in range(1, n_col)
        ]
        for one in parts_:
            one.start()
        for one in parts_:
            one.wait()
        added = total_of(scol)
    loss = 0.5 * jnp.sum(added[0:1], keepdims=True)
    image_norm = jnp.sum(added[1:2], keepdims=True)
    kernel_norm = jnp.sum(added[2:3], keepdims=True)
    refined[...] = wide[near, :tile_cols] - refined[...] * (loss / (image_norm + EPSILON))
    rate = 0.25 * loss / (kernel_norm + EPSILON)
    for one in gathers:
        one.wait()
    for c in range(n_col):
        rows = slice(c * few, (c + 1) * few)
        new_kernel[rows, :] = own[rows, :] - pieces[c] * rate
    for k in range(2 * pairs - 1):
        gather(k).wait_send()
    for i in range(8):

        @pl.when(target_of(i))
        def _():
            halo(i, estimate, wide, hs, hr).wait_send()
            halo(i, wider, wider, bs, br).wait_send()


def leave(refined, new_kernel, refined_out, kernel_out, sem):
    moves = [
        pltpu.make_async_copy(refined, refined_out, sem.at[0]),
        pltpu.make_async_copy(new_kernel, kernel_out, sem.at[1]),
    ]
    for one in moves:
        one.start()
    for one in moves:
        one.wait()


def split(x):
    high = np.asarray(x, np.float32).astype(jnp.bfloat16)
    low = (np.asarray(x, np.float32) - high.astype(np.float32)).astype(jnp.bfloat16)
    return jnp.asarray(np.stack([high, low]))


def make_tables(n_row, owner, side):
    margin = side // 2
    wide, tall = 3 * side, 2 * side
    scale = 2.0 / (wide * tall) / side
    inside, centred = np.arange(side), np.arange(side) - margin

    def waves(places, freqs, period):
        phase = np.mod(np.outer(places, freqs), period) * (2 * math.pi / period)
        return np.cos(phase), np.sin(phase)

    first, second = 6 * np.arange(side) + 1, 6 * np.arange(margin) + 3

    def line_table(places):
        c0, s0 = waves(places, first, 2 * wide)
        c1, s1 = waves(places, second, 2 * wide)
        return np.concatenate([c0, -s0, c1, -s1], axis=1)

    c0, s0 = waves(inside, first, 2 * wide)
    c1, s1 = waves(inside, second, 2 * wide)
    own_fwd = np.block([[c0, -s0], [s0, c0]])
    own_fwd1 = np.concatenate([c1, -s1], axis=1)
    beside = np.concatenate([2 * side + np.arange(margin), np.arange(margin) - margin])

    def row_table(places):
        j = np.arange(margin)
        ce, se = waves(2 * j, places, tall)
        se[0] = np.cos(math.pi * places)
        co, so = waves(2 * j + 1, places, tall)
        return np.concatenate([ce, se, co, so], axis=0)

    blocks = list(range(0, n_row, 2)) + list(range(1, n_row, 2))
    turned = np.concatenate([np.arange(r * owner, (r + 1) * owner) for r in blocks])
    lag = line_table(centred)
    return [
        split(x)
        for x in (
            lag, lag.T * scale, own_fwd, own_fwd1, line_table(beside), own_fwd.T * scale,
            own_fwd1.T * scale, row_table(centred), row_table(inside), row_table(inside).T,
            row_table(centred).T[turned],
        )
    ]


def per_device(n_row, n_col, observed, estimate, kernel):
    tile_rows, tile_cols = observed.shape
    owner, side = kernel.shape
    margin = side // 2
    rows_long, cols_long = tile_rows + side, tile_cols + side
    tables = make_tables(n_row, owner, side)
    dma = pltpu.SemaphoreType.DMA
    more_c = max(n_col - 1, 1)
    few = owner // n_col
    pairs = n_row // 2
    firsts = n_row * n_col if n_row * n_col <= FEW else n_row
    spectrum = VMEM((rows_long, cols_long), F32)
    more_p = max(pairs * n_col - 1, 1)
    outs = pl.pallas_call(
        functools.partial(body, n_row, n_col),
        out_shape=(
            VMEM((tile_rows, tile_cols), F32),
            VMEM((owner, side), F32),
        ),
        in_specs=[pl.BlockSpec(memory_space=pl.ANY)] * (3 + len(tables)),
        out_specs=(pl.BlockSpec(memory_space=VMEM),) * 2,
        scratch_shapes=[VMEM(x.shape, BF16) for x in tables] + [
            spectrum,
            spectrum,
            VMEM((tile_rows, tile_cols), F32),
            VMEM((owner, side), F32),
            VMEM((side, side), F32),
            VMEM((tile_rows, cols_long), F32),
            spectrum,
            spectrum,
            spectrum,
            VMEM((2, rows_long, cols_long), BF16),
            VMEM((side, side), F32),
            VMEM((margin, side), F32),
            VMEM((pairs * n_col, few, side), F32),
            VMEM((more_p, few, side), F32),
            VMEM((n_col, few, side), F32),
            VMEM((firsts, 8, 128), F32),
            VMEM((n_col, 8, 128), F32),
            VMEM((8, 128), F32),
            dma((3 + len(tables),)),
            dma((8,)), dma((8,)),
            dma((n_row,)), dma((n_row,)),
            dma((8,)), dma((8,)),
            dma((2,)),
            dma((more_p,)), dma((more_p,)),
            dma((more_c,)), dma((more_c,)),
            dma((firsts,)), dma((firsts,)),
            dma((more_c,)), dma((more_c,)),
        ],
        compiler_params=pltpu.CompilerParams(
            collective_id=0, has_side_effects=True, vmem_limit_bytes=56 * 1024 * 1024
        ),
        name="deconvolve",
    )(observed, estimate, kernel, *tables)
    return pl.pallas_call(
        leave,
        out_shape=tuple(jax.ShapeDtypeStruct(x.shape, F32) for x in (observed, kernel)),
        in_specs=[pl.BlockSpec(memory_space=VMEM)] * 2,
        out_specs=(pl.BlockSpec(memory_space=pl.ANY),) * 2,
        scratch_shapes=[dma((2,))],
        name="leave",
    )(*[pltpu.with_memory_space_constraint(x, VMEM) for x in outs])


def solution(mesh):
    placed = (P(("groups", "row"), "col"), P(("groups", "row"), "col"), P(("groups", "row"), None))
    return jax.shard_map(
        functools.partial(per_device, mesh.shape["row"], mesh.shape["col"]),
        mesh=mesh,
        in_specs=placed,
        out_specs=(P(("groups", "row"), "col"), P(("groups", "row"), None)),
        check_vma=False,
    )
```

```python
import functools
import math

import jax
import jax.numpy as jnp
import numpy as np
from jax import lax
from jax.experimental import pallas as pl
from jax.experimental.pallas import tpu as pltpu
from jax.sharding import PartitionSpec as P

EPSILON = 1e-06
MESH = pl.DeviceIdType.MESH
FEW = 16
VMEM = pltpu.VMEM
BF16 = jnp.bfloat16
F32 = jnp.float32
ROOT = math.sqrt(3.0) / 2.0
AROUND = [(a, b) for a in (-1, 0, 1) for b in (-1, 0, 1) if (a, b) != (0, 0)]
SIDES = [i for i, (a, b) in enumerate(AROUND) if a * b == 0]
CORNERS = [i for i, (a, b) in enumerate(AROUND) if a * b != 0]


def here(row, col, n_row, n_col):
    return (row >= 0) & (row < n_row) & (col >= 0) & (col < n_col)


def others(n_row, n_col):
    return [(s, t) for s in range(n_row) for t in range(n_col) if (s, t) != (0, 0)]


def peer(row, col, s, t, n_row, n_col):
    return {"row": lax.rem(row + s, n_row), "col": lax.rem(col + t, n_col)}


def spans(tile, margin):
    inner = {-1: (0, margin), 0: (0, tile), 1: (tile - margin, margin)}
    outer = {-1: (tile + margin, margin), 0: (0, tile), 1: (tile, margin)}
    return inner, outer


def at(ref, rows, cols):
    return ref.at[pl.ds(*rows), pl.ds(*cols)]


def line(x):
    rows, cols = x.shape
    if rows % 8:
        x = jnp.concatenate([x, jnp.zeros((8 - rows % 8, cols), F32)], axis=0)
        rows = x.shape[0]
    x = (x * x).reshape(rows // 8, 8, cols).sum(axis=0)
    total = x[:, :128]
    for at_col in range(128, cols, 128):
        total = total + x[:, at_col : at_col + 128]
    return jnp.sum(total, axis=0, keepdims=True)


def halves(x):
    high = x.astype(BF16)
    return high, (x - high.astype(F32)).astype(BF16)


def dot3(a, b):
    dot = lambda p, q: lax.dot_general(p, q, (((1,), (0,)), ((), ())), preferred_element_type=F32)
    return dot(a[0], b[0]) + (dot(a[0], b[1]) + dot(a[1], b[0]))


def body(
    n_row, n_col, observed, estimate, kernel, *rest
):
    tables, rest = rest[:11], rest[11:]
    refined, new_kernel = rest[:2]
    held, rest = rest[2:13], rest[13:]
    (wide, wider, obs, own, full, near_t, far_t, spec_i, spec_k, mixed, kgrad, pland,
     cpart, cland, pieces, srow, scol, sums, *sems) = rest
    (ls, hs, hr, ks, kr, bs, br, ps, cs, cr, gs, gr, as_, ar, es, er) = sems
    (lag_fwd, lag_inv, own_fwd, own_fwd1, side_fwd, own_inv, own_inv1,
     row_lag, row_own, inv_own, inv_lag) = held
    row, col = lax.axis_index("row"), lax.axis_index("col")
    tile_rows, tile_cols = observed.shape
    owner, side = kernel.shape
    margin = side // 2
    rows_long, cols_long = tile_rows + side, tile_cols + side
    in_r, out_r = spans(tile_rows, margin)
    in_c, out_c = spans(tile_cols, margin)
    pairs = n_row // 2
    core = lax.rem(row, 2)
    twin = row + 1 - 2 * core
    few = owner // n_col

    def copy(src, dst, ssem, rsem, **target):
        return pltpu.make_async_remote_copy(
            src_ref=src, dst_ref=dst, send_sem=ssem, recv_sem=rsem,
            device_id=target, device_id_type=MESH,
        )

    def halo(i, src, dst, ssem, rsem):
        dr, dc = AROUND[i]
        return copy(
            at(src, in_r[dr], in_c[dc]), at(dst, out_r[-dr], out_c[-dc]),
            ssem.at[i], rsem.at[i], row=row + dr, col=col + dc,
        )

    def target_of(i):
        dr, dc = AROUND[i]
        return here(row + dr, col + dc, n_row, n_col)

    def source_of(i):
        dr, dc = AROUND[i]
        return here(row - dr, col - dc, n_row, n_col)

    def block(r):
        return pl.ds(pl.multiple_of(r * owner, owner), owner)

    barrier = pltpu.get_barrier_semaphore()
    for s, t in sorted(others(n_row, n_col), key=lambda o: min(o[0], n_row - o[0]) + min(o[1], n_col - o[1])):
        pl.semaphore_signal(
            barrier, inc=1, device_id=peer(row, col, s, t, n_row, n_col), device_id_type=MESH
        )
    near, far = slice(0, tile_rows), slice(tile_rows, rows_long)
    loads = [
        pltpu.make_async_copy(estimate, wide.at[near, :tile_cols], ls.at[0]),
        pltpu.make_async_copy(kernel, own, ls.at[1]),
        pltpu.make_async_copy(observed, obs, ls.at[2]),
    ]
    order = (2, 3, 0, 7, 4, 8, 9, 5, 6, 10, 1)
    fetch = {
        k: pltpu.make_async_copy(tables[k], held[k], ls.at[3 + k]) for k in order
    }
    for one in loads[:2]:
        one.start()
    pl.semaphore_wait(barrier, n_row * n_col - 1)
    for one in loads[:2]:
        one.wait()

    def gather(k):
        if k == 0:
            return copy(own, full.at[block(row), :], ks.at[0], kr.at[0], row=twin)
        if k < pairs:
            there = lax.rem(row + 2 * k, n_row)
            return copy(own, full.at[block(row), :], ks.at[k], kr.at[k], row=there)
        behind = lax.rem(row + n_row - 2 * (k - pairs + 1), n_row)
        return copy(
            full.at[block(behind), :], full.at[block(behind), :], ks.at[k], kr.at[k], row=twin
        )

    def send(src, dst, ssem, rsem):
        for i in SIDES + CORNERS:

            @pl.when(target_of(i))
            def _():
                halo(i, src, dst, ssem, rsem).start()

    def receive(some, src, dst, ssem, rsem):
        for i in some:

            @pl.when(source_of(i))
            def _():
                halo(i, src, dst, ssem, rsem).wait_recv()

    for k in range(pairs):
        gather(k).start()
    send(wide, wide, hs, hr)
    loads[2].start()
    for k in order:
        fetch[k].start()

    for i, (dr, dc) in enumerate(AROUND):

        @pl.when(jnp.logical_not(source_of(i)))
        def _():
            empty = jnp.zeros((out_r[-dr][1], out_c[-dc][1]), F32)
            wide[pl.ds(*out_r[-dr]), pl.ds(*out_c[-dc])] = empty
            wider[pl.ds(*out_r[-dr]), pl.ds(*out_c[-dc])] = empty

    def pair(ref, rows=slice(None), cols=slice(None)):
        return ref[0, rows, cols], ref[1, rows, cols]

    def three(x):
        return x[:, :side], x[:, side : 2 * side]

    groups = (
        (slice(0, 2 * side), slice(0, side), slice(side, 2 * side)),
        (slice(2 * side, 3 * side), slice(2 * side, 2 * side + margin), slice(2 * side + margin, 3 * side)),
    )

    def columns(x0, x1):
        u, v, w = x0 + 0.5 * x1, -ROOT * x1, x0 - x1
        return (
            dot3(halves(jnp.concatenate([u, v], axis=1)), pair(own_fwd)),
            dot3(halves(w), pair(own_fwd1)),
        )

    def rows_of(table, even, odd):
        return (
            dot3(pair(table, slice(0, side)), even),
            dot3(pair(table, slice(side, 2 * side)), odd),
        )

    def unfold(g, outs, spec, other, conj):
        step = 16
        every, re, im = groups[g]
        half = re.stop - re.start
        for base, out in zip((0, side), outs):
            for k in range(margin // step):
                here_ = slice(k * step, (k + 1) * step)
                there = slice(margin + k * step, margin + (k + 1) * step)
                up = slice(base + k * step, base + (k + 1) * step)
                down = slice(base + margin + k * step, base + margin + (k + 1) * step)
                first = None
                if base == 0 and k == 0:
                    first = lax.broadcasted_iota(jnp.int32, (step, half), 0) == 0
                pr, pi, qr, qi = out[here_, :half], out[here_, half:], out[there, :half], out[there, half:]
                ur, ui, dr, di = pr + qi, pi - qr, pr - qi, pi + qr
                if first is not None:
                    ur, ui = jnp.where(first, pr, ur), jnp.where(first, pi, ui)
                    dr, di = jnp.where(first, qr, dr), jnp.where(first, qi, di)
                if spec is not None:
                    spec[up, re], spec[up, im] = ur, ui
                    spec[down, re], spec[down, im] = dr, di
                if other is None:
                    continue
                both = []
                for rows, xr, xi in ((up, ur, ui), (down, dr, di)):
                    yr, yi = other[rows, re], other[rows, im]
                    if conj:
                        both.append((xr * yr + xi * yi, xi * yr - xr * yi))
                    else:
                        both.append((xr * yr - xi * yi, xr * yi + xi * yr))
                (ur, ui), (dr, di) = both
                cr_, ci_, sr_, si_ = ur + dr, ui + di, di - ui, ur - dr
                if first is not None:
                    cr_, ci_ = jnp.where(first, ur, cr_), jnp.where(first, ui, ci_)
                    sr_, si_ = jnp.where(first, dr, sr_), jnp.where(first, di, si_)
                for rows, cols, v in ((up, re, cr_), (up, im, ci_), (down, re, sr_), (down, im, si_)):
                    high, low = halves(v)
                    mixed[0, rows, cols] = high
                    mixed[1, rows, cols] = low

    def own_columns(ref):
        for (every, _, _), part in zip(groups, columns(*three(ref[near, :tile_cols]))):
            near_t[:, every] = part

    def outer_columns(ref):
        aside = halves(ref[near, tile_cols:])
        below = columns(*three(ref[far, :tile_cols]))
        for (every, _, _), part in zip(groups, below):
            near_t[:, every] = near_t[:, every] + dot3(aside, pair(side_fwd, cols=every))
            far_t[:, every] = part

    def spectrum_of(ref):
        corner = halves(ref[far, tile_cols:])
        outs = []
        for every, _, _ in groups:
            beside = near_t[:, every]
            below = far_t[:, every] + dot3(corner, pair(side_fwd, cols=every))
            outs.append(rows_of(row_own, halves(beside + below), halves(beside - below)))
        return outs

    def rows_back(table, outs, spec, other, conj):
        back = []
        for g in (0, 1):
            unfold(g, outs[g], spec, other, conj)
            back.append(dot3(pair(table), pair(mixed, cols=groups[g][0])))
        return back

    def own_values(back):
        v = dot3(halves(back[0]), pair(own_inv))
        w = dot3(halves(back[1]), pair(own_inv1))
        vr, vi = v[:, :side], v[:, side:]
        return vr + w, 0.5 * vr - ROOT * vi - w

    fetch[2].wait()
    fetch[3].wait()
    own_columns(wide)

    full[block(row), :] = own[...]
    for k in range(1, pairs):
        gather(k).wait_recv()
        gather(k + pairs - 1).start()
    gather(0).wait_recv()
    for k in range(pairs, 2 * pairs - 1):
        gather(k).wait_recv()
    fetch[0].wait()
    fetch[7].wait()
    turned = halves(full[...])
    for g in (0, 1):
        lines = halves(dot3(turned, pair(lag_fwd, cols=groups[g][0])))
        unfold(g, rows_of(row_lag, lines, lines), spec_k, None, False)

    for k in (1, 4, 5, 6, 8, 9, 10):
        fetch[k].wait()
    loads[2].wait()
    receive(SIDES, wide, wide, hs, hr)
    outer_columns(wide)
    receive(CORNERS, wide, wide, hs, hr)
    x0, x1 = own_values(rows_back(inv_own, spectrum_of(wide), spec_i, spec_k, False))
    x0, x1 = x0 - obs[:, :side], x1 - obs[:, side:]
    wider[near, :side] = x0
    wider[near, side:tile_cols] = x1
    send(wider, wider, bs, br)
    sums[...] = jnp.zeros_like(sums)
    sums[0:1] = line(x0) + line(x1)
    own_columns(wider)
    outs = []
    for every, _, _ in groups:
        lines = halves(near_t[:, every])
        outs.append(rows_of(row_own, lines, lines))
    back = rows_back(inv_lag, outs, None, spec_i, True)
    kgrad[...] = dot3(halves(jnp.concatenate(back, axis=1)), pair(lag_inv))

    def share(c):
        return pl.ds(pl.multiple_of(c * margin, margin), margin)

    swap = copy(kgrad.at[share(1 - core), :], pland, ps.at[0], ps.at[1], row=twin)
    swap.start()
    swap.wait()
    mine = kgrad[share(core), :] + pland[...]
    for k in range(pairs * n_col):
        cpart[k] = mine[k * few : (k + 1) * few]
    half_row = row // 2
    scatter = []
    for s, t in others(pairs, n_col):
        r, c = lax.rem(half_row + s, pairs), lax.rem(col + t, n_col)
        k = s * n_col + t - 1
        scatter.append(copy(
            cpart.at[r * n_col + c], cland.at[k], cs.at[k], cr.at[k], row=2 * r + core, col=c
        ))
    for one in scatter:
        one.start()

    for k in range(2 * pairs - 1):
        gather(k).wait_send()
    for i in range(8):

        @pl.when(target_of(i))
        def _():
            halo(i, wide, wide, hs, hr).wait_send()

    receive(SIDES, wider, wider, bs, br)
    outer_columns(wider)
    receive(CORNERS, wider, wider, bs, br)
    x0, x1 = own_values(rows_back(inv_own, spectrum_of(wider), None, spec_k, True))
    refined[:, :side] = x0
    refined[:, side:] = x1
    sums[1:2] = line(x0) + line(x1)

    for i in range(8):

        @pl.when(target_of(i))
        def _():
            halo(i, wider, wider, bs, br).wait_send()

    piece = cpart[half_row * n_col + col]
    for k, one in enumerate(scatter):
        one.wait()
        piece = piece + cland[k]
    pieces[col] = piece
    sums[2:3] = line(piece)
    gathers = [
        copy(pieces.at[col], pieces.at[col], gs.at[s - 1], gr.at[s - 1], col=lax.rem(col + s, n_col))
        for s in range(1, n_col)
    ]

    def total_of(buf):
        added = buf[0]
        for k in range(1, buf.shape[0]):
            added = added + buf[k]
        return added

    if n_row * n_col <= FEW:
        me = row * n_col + col
        srow[me] = sums[...]
        parts_ = [
            copy(srow.at[me], srow.at[me], as_.at[k], ar.at[k], **peer(row, col, s, t, n_row, n_col))
            for k, (s, t) in enumerate(others(n_row, n_col))
        ]
        for one in parts_ + gathers:
            one.start()
        for one in parts_:
            one.wait()
        added = total_of(srow)
    else:
        srow[row] = sums[...]
        parts_ = [
            copy(srow.at[row], srow.at[row], as_.at[s - 1], ar.at[s - 1], row=lax.rem(row + s, n_row))
            for s in range(1, n_row)
        ]
        for one in parts_ + gathers:
            one.start()
        for one in parts_:
            one.wait()
        scol[col] = total_of(srow)
        parts_ = [
            copy(scol.at[col], scol.at[col], es.at[s - 1], er.at[s - 1], col=lax.rem(col + s, n_col))
            for s in range(1, n_col)
        ]
        for one in parts_:
            one.start()
        for one in parts_:
            one.wait()
        added = total_of(scol)
    loss = 0.5 * jnp.sum(added[0:1], keepdims=True)
    image_norm = jnp.sum(added[1:2], keepdims=True)
    kernel_norm = jnp.sum(added[2:3], keepdims=True)
    refined[...] = wide[near, :tile_cols] - refined[...] * (loss / (image_norm + EPSILON))
    rate = 0.25 * loss / (kernel_norm + EPSILON)
    for one in gathers:
        one.wait()
    for c in range(n_col):
        rows = slice(c * few, (c + 1) * few)
        new_kernel[rows, :] = own[rows, :] - pieces[c] * rate


def leave(refined, new_kernel, refined_out, kernel_out, sem):
    moves = [
        pltpu.make_async_copy(refined, refined_out, sem.at[0]),
        pltpu.make_async_copy(new_kernel, kernel_out, sem.at[1]),
    ]
    for one in moves:
        one.start()
    for one in moves:
        one.wait()


def split(x):
    high = np.asarray(x, np.float32).astype(jnp.bfloat16)
    low = (np.asarray(x, np.float32) - high.astype(np.float32)).astype(jnp.bfloat16)
    return jnp.asarray(np.stack([high, low]))


def make_tables(n_row, owner, side):
    margin = side // 2
    wide, tall = 3 * side, 2 * side
    scale = 2.0 / (wide * tall) / side
    inside, centred = np.arange(side), np.arange(side) - margin

    def waves(places, freqs, period):
        phase = np.mod(np.outer(places, freqs), period) * (2 * math.pi / period)
        return np.cos(phase), np.sin(phase)

    first, second = 6 * np.arange(side) + 1, 6 * np.arange(margin) + 3

    def line_table(places):
        c0, s0 = waves(places, first, 2 * wide)
        c1, s1 = waves(places, second, 2 * wide)
        return np.concatenate([c0, -s0, c1, -s1], axis=1)

    c0, s0 = waves(inside, first, 2 * wide)
    c1, s1 = waves(inside, second, 2 * wide)
    own_fwd = np.block([[c0, -s0], [s0, c0]])
    own_fwd1 = np.concatenate([c1, -s1], axis=1)
    beside = np.concatenate([2 * side + np.arange(margin), np.arange(margin) - margin])

    def row_table(places):
        j = np.arange(margin)
        ce, se = waves(2 * j, places, tall)
        se[0] = np.cos(math.pi * places)
        co, so = waves(2 * j + 1, places, tall)
        return np.concatenate([ce, se, co, so], axis=0)

    blocks = list(range(0, n_row, 2)) + list(range(1, n_row, 2))
    turned = np.concatenate([np.arange(r * owner, (r + 1) * owner) for r in blocks])
    lag = line_table(centred)
    return [
        split(x)
        for x in (
            lag, lag.T * scale, own_fwd, own_fwd1, line_table(beside), own_fwd.T * scale,
            own_fwd1.T * scale, row_table(centred), row_table(inside), row_table(inside).T,
            row_table(centred).T[turned],
        )
    ]


def per_device(n_row, n_col, observed, estimate, kernel):
    tile_rows, tile_cols = observed.shape
    owner, side = kernel.shape
    margin = side // 2
    rows_long, cols_long = tile_rows + side, tile_cols + side
    tables = make_tables(n_row, owner, side)
    dma = pltpu.SemaphoreType.DMA
    more_c = max(n_col - 1, 1)
    few = owner // n_col
    pairs = n_row // 2
    firsts = n_row * n_col if n_row * n_col <= FEW else n_row
    spectrum = VMEM((rows_long, cols_long), F32)
    more_p = max(pairs * n_col - 1, 1)
    outs = pl.pallas_call(
        functools.partial(body, n_row, n_col),
        out_shape=(
            VMEM((tile_rows, tile_cols), F32),
            VMEM((owner, side), F32),
        ),
        in_specs=[pl.BlockSpec(memory_space=pl.ANY)] * (3 + len(tables)),
        out_specs=(pl.BlockSpec(memory_space=VMEM),) * 2,
        scratch_shapes=[VMEM(x.shape, BF16) for x in tables] + [
            spectrum,
            spectrum,
            VMEM((tile_rows, tile_cols), F32),
            VMEM((owner, side), F32),
            VMEM((side, side), F32),
            VMEM((tile_rows, cols_long), F32),
            VMEM((side, cols_long), F32),
            spectrum,
            spectrum,
            VMEM((2, rows_long, cols_long), BF16),
            VMEM((side, side), F32),
            VMEM((margin, side), F32),
            VMEM((pairs * n_col, few, side), F32),
            VMEM((more_p, few, side), F32),
            VMEM((n_col, few, side), F32),
            VMEM((firsts, 8, 128), F32),
            VMEM((n_col, 8, 128), F32),
            VMEM((8, 128), F32),
            dma((3 + len(tables),)),
            dma((8,)), dma((8,)),
            dma((n_row,)), dma((n_row,)),
            dma((8,)), dma((8,)),
            dma((2,)),
            dma((more_p,)), dma((more_p,)),
            dma((more_c,)), dma((more_c,)),
            dma((firsts,)), dma((firsts,)),
            dma((more_c,)), dma((more_c,)),
        ],
        compiler_params=pltpu.CompilerParams(
            collective_id=0, has_side_effects=True, vmem_limit_bytes=56 * 1024 * 1024
        ),
        name="deconvolve",
    )(observed, estimate, kernel, *tables)
    return pl.pallas_call(
        leave,
        out_shape=tuple(jax.ShapeDtypeStruct(x.shape, F32) for x in (observed, kernel)),
        in_specs=[pl.BlockSpec(memory_space=VMEM)] * 2,
        out_specs=(pl.BlockSpec(memory_space=pl.ANY),) * 2,
        scratch_shapes=[dma((2,))],
        name="leave",
    )(*[pltpu.with_memory_space_constraint(x, VMEM) for x in outs])


def solution(mesh):
    placed = (P(("groups", "row"), "col"), P(("groups", "row"), "col"), P(("groups", "row"), None))
    return jax.shard_map(
        functools.partial(per_device, mesh.shape["row"], mesh.shape["col"]),
        mesh=mesh,
        in_specs=placed,
        out_specs=(P(("groups", "row"), "col"), P(("groups", "row"), None)),
        check_vma=False,
    )
```

```python
import functools
import math

import jax
import jax.numpy as jnp
import numpy as np
from jax import lax
from jax.experimental import pallas as pl
from jax.experimental.pallas import tpu as pltpu
from jax.sharding import PartitionSpec as P

EPSILON = 1e-06
MESH = pl.DeviceIdType.MESH
FEW = 16
VMEM = pltpu.VMEM
BF16 = jnp.bfloat16
F32 = jnp.float32
ROOT = math.sqrt(3.0) / 2.0
AROUND = [(a, b) for a in (-1, 0, 1) for b in (-1, 0, 1) if (a, b) != (0, 0)]
SIDES = [i for i, (a, b) in enumerate(AROUND) if a * b == 0]
LEVEL = [i for i, (a, b) in enumerate(AROUND) if a == 0]
UPRIGHT = [i for i, (a, b) in enumerate(AROUND) if b == 0]
CORNERS = [i for i, (a, b) in enumerate(AROUND) if a * b != 0]


def here(row, col, n_row, n_col):
    return (row >= 0) & (row < n_row) & (col >= 0) & (col < n_col)


def others(n_row, n_col):
    return [(s, t) for s in range(n_row) for t in range(n_col) if (s, t) != (0, 0)]


def peer(row, col, s, t, n_row, n_col):
    return {"row": lax.rem(row + s, n_row), "col": lax.rem(col + t, n_col)}


def spans(tile, margin):
    inner = {-1: (0, margin), 0: (0, tile), 1: (tile - margin, margin)}
    outer = {-1: (tile + margin, margin), 0: (0, tile), 1: (tile, margin)}
    return inner, outer


def at(ref, rows, cols):
    return ref.at[pl.ds(*rows), pl.ds(*cols)]


def line(x):
    rows, cols = x.shape
    if rows % 8:
        x = jnp.concatenate([x, jnp.zeros((8 - rows % 8, cols), F32)], axis=0)
        rows = x.shape[0]
    x = (x * x).reshape(rows // 8, 8, cols).sum(axis=0)
    total = x[:, :128]
    for at_col in range(128, cols, 128):
        total = total + x[:, at_col : at_col + 128]
    return jnp.sum(total, axis=0, keepdims=True)


def halves(x):
    high = x.astype(BF16)
    return high, (x - high.astype(F32)).astype(BF16)


def dot3(a, b):
    dot = lambda p, q: lax.dot_general(p, q, (((1,), (0,)), ((), ())), preferred_element_type=F32)
    return dot(a[0], b[0]) + (dot(a[0], b[1]) + dot(a[1], b[0]))


def body(
    n_row, n_col, observed, estimate, kernel, *rest
):
    tables, rest = rest[:11], rest[11:]
    refined, new_kernel = rest[:2]
    held, rest = rest[2:13], rest[13:]
    (wide, wider, obs, own, full, near_t, far_t, spec_i, spec_k, mixed, kgrad, pland,
     cpart, cland, pieces, srow, scol, sums, *sems) = rest
    (ls, hs, hr, ks, kr, bs, br, ps, cs, cr, gs, gr, as_, ar, es, er) = sems
    (lag_fwd, lag_inv, own_fwd, own_fwd1, side_fwd, own_inv, own_inv1,
     row_lag, row_own, inv_own, inv_lag) = held
    row, col = lax.axis_index("row"), lax.axis_index("col")
    tile_rows, tile_cols = observed.shape
    owner, side = kernel.shape
    margin = side // 2
    rows_long, cols_long = tile_rows + side, tile_cols + side
    in_r, out_r = spans(tile_rows, margin)
    in_c, out_c = spans(tile_cols, margin)
    pairs = n_row // 2
    core = lax.rem(row, 2)
    twin = row + 1 - 2 * core
    few = owner // n_col

    def copy(src, dst, ssem, rsem, **target):
        return pltpu.make_async_remote_copy(
            src_ref=src, dst_ref=dst, send_sem=ssem, recv_sem=rsem,
            device_id=target, device_id_type=MESH,
        )

    def halo(i, src, dst, ssem, rsem):
        dr, dc = AROUND[i]
        return copy(
            at(src, in_r[dr], in_c[dc]), at(dst, out_r[-dr], out_c[-dc]),
            ssem.at[i], rsem.at[i], row=row + dr, col=col + dc,
        )

    def target_of(i):
        dr, dc = AROUND[i]
        return here(row + dr, col + dc, n_row, n_col)

    def source_of(i):
        dr, dc = AROUND[i]
        return here(row - dr, col - dc, n_row, n_col)

    def block(r):
        return pl.ds(pl.multiple_of(r * owner, owner), owner)

    barrier = pltpu.get_barrier_semaphore()
    for s, t in sorted(others(n_row, n_col), key=lambda o: min(o[0], n_row - o[0]) + min(o[1], n_col - o[1])):
        pl.semaphore_signal(
            barrier, inc=1, device_id=peer(row, col, s, t, n_row, n_col), device_id_type=MESH
        )
    near, far = slice(0, tile_rows), slice(tile_rows, rows_long)
    loads = [
        pltpu.make_async_copy(estimate, wide.at[near, :tile_cols], ls.at[0]),
        pltpu.make_async_copy(kernel, own, ls.at[1]),
        pltpu.make_async_copy(observed, obs, ls.at[2]),
    ]
    order = (2, 3, 0, 7, 4, 8, 9, 5, 6, 10, 1)
    fetch = {
        k: pltpu.make_async_copy(tables[k], held[k], ls.at[3 + k]) for k in order
    }
    for one in loads[:2]:
        one.start()
    pl.semaphore_wait(barrier, n_row * n_col - 1)
    for one in loads[:2]:
        one.wait()

    def gather(k):
        if k == 0:
            return copy(own, full.at[block(row), :], ks.at[0], kr.at[0], row=twin)
        if k < pairs:
            there = lax.rem(row + 2 * k, n_row)
            return copy(own, full.at[block(row), :], ks.at[k], kr.at[k], row=there)
        behind = lax.rem(row + n_row - 2 * (k - pairs + 1), n_row)
        return copy(
            full.at[block(behind), :], full.at[block(behind), :], ks.at[k], kr.at[k], row=twin
        )

    def send(src, dst, ssem, rsem):
        for i in SIDES + CORNERS:

            @pl.when(target_of(i))
            def _():
                halo(i, src, dst, ssem, rsem).start()

    def receive(some, src, dst, ssem, rsem):
        for i in some:

            @pl.when(source_of(i))
            def _():
                halo(i, src, dst, ssem, rsem).wait_recv()

    for k in range(pairs):
        gather(k).start()
    send(wide, wide, hs, hr)
    loads[2].start()
    for k in order:
        fetch[k].start()

    for i, (dr, dc) in enumerate(AROUND):

        @pl.when(jnp.logical_not(source_of(i)))
        def _():
            empty = jnp.zeros((out_r[-dr][1], out_c[-dc][1]), F32)
            wide[pl.ds(*out_r[-dr]), pl.ds(*out_c[-dc])] = empty
            wider[pl.ds(*out_r[-dr]), pl.ds(*out_c[-dc])] = empty

    def pair(ref, rows=slice(None), cols=slice(None)):
        return ref[0, rows, cols], ref[1, rows, cols]

    def three(x):
        return x[:, :side], x[:, side : 2 * side]

    groups = (
        (slice(0, 2 * side), slice(0, side), slice(side, 2 * side)),
        (slice(2 * side, 3 * side), slice(2 * side, 2 * side + margin), slice(2 * side + margin, 3 * side)),
    )

    def columns(x0, x1):
        u, v, w = x0 + 0.5 * x1, -ROOT * x1, x0 - x1
        return (
            dot3(halves(jnp.concatenate([u, v], axis=1)), pair(own_fwd)),
            dot3(halves(w), pair(own_fwd1)),
        )

    def rows_of(table, even, odd):
        return (
            dot3(pair(table, slice(0, side)), even),
            dot3(pair(table, slice(side, 2 * side)), odd),
        )

    def unfold(g, outs, spec, other, conj):
        step = 16
        every, re, im = groups[g]
        half = re.stop - re.start
        for base, out in zip((0, side), outs):
            for k in range(margin // step):
                here_ = slice(k * step, (k + 1) * step)
                there = slice(margin + k * step, margin + (k + 1) * step)
                up = slice(base + k * step, base + (k + 1) * step)
                down = slice(base + margin + k * step, base + margin + (k + 1) * step)
                first = None
                if base == 0 and k == 0:
                    first = lax.broadcasted_iota(jnp.int32, (step, half), 0) == 0
                pr, pi, qr, qi = out[here_, :half], out[here_, half:], out[there, :half], out[there, half:]
                ur, ui, dr, di = pr + qi, pi - qr, pr - qi, pi + qr
                if first is not None:
                    ur, ui = jnp.where(first, pr, ur), jnp.where(first, pi, ui)
                    dr, di = jnp.where(first, qr, dr), jnp.where(first, qi, di)
                if spec is not None:
                    spec[up, re], spec[up, im] = ur, ui
                    spec[down, re], spec[down, im] = dr, di
                if other is None:
                    continue
                both = []
                for rows, xr, xi in ((up, ur, ui), (down, dr, di)):
                    yr, yi = other[rows, re], other[rows, im]
                    if conj:
                        both.append((xr * yr + xi * yi, xi * yr - xr * yi))
                    else:
                        both.append((xr * yr - xi * yi, xr * yi + xi * yr))
                (ur, ui), (dr, di) = both
                cr_, ci_, sr_, si_ = ur + dr, ui + di, di - ui, ur - dr
                if first is not None:
                    cr_, ci_ = jnp.where(first, ur, cr_), jnp.where(first, ui, ci_)
                    sr_, si_ = jnp.where(first, dr, sr_), jnp.where(first, di, si_)
                for rows, cols, v in ((up, re, cr_), (up, im, ci_), (down, re, sr_), (down, im, si_)):
                    high, low = halves(v)
                    mixed[0, rows, cols] = high
                    mixed[1, rows, cols] = low

    def own_columns(ref):
        for (every, _, _), part in zip(groups, columns(*three(ref[near, :tile_cols]))):
            near_t[:, every] = part

    def outer_columns(ref):
        aside = halves(ref[near, tile_cols:])
        below = columns(*three(ref[far, :tile_cols]))
        for (every, _, _), part in zip(groups, below):
            near_t[:, every] = near_t[:, every] + dot3(aside, pair(side_fwd, cols=every))
            far_t[:, every] = part

    def spectrum_of(ref):
        corner = halves(ref[far, tile_cols:])
        outs = []
        for every, _, _ in groups:
            beside = near_t[:, every]
            below = far_t[:, every] + dot3(corner, pair(side_fwd, cols=every))
            outs.append(rows_of(row_own, halves(beside + below), halves(beside - below)))
        return outs

    def half(which):
        return pl.ds(pl.multiple_of(margin * (which + core - 2 * which * core), margin), margin)

    def side_half(i, which):
        dc = AROUND[i][1]
        k = i + 5 * which
        return copy(
            wider.at[half(which), pl.ds(*in_c[dc])], wider.at[half(which), pl.ds(*out_c[-dc])],
            bs.at[k], br.at[k], row=row, col=col + dc,
        )

    def outward(i):
        dr = AROUND[i][0]
        return core == (1 if dr == 1 else 0)

    def send_half(which):
        for i in UPRIGHT + LEVEL + CORNERS:
            level = i in LEVEL
            there = target_of(i)
            if not level:
                there = there & (outward(i) if which == 0 else jnp.logical_not(outward(i)))

            @pl.when(there)
            def _():
                (side_half(i, which) if level else halo(i, wider, wider, bs, br)).start()

    def receive_sides():
        receive(UPRIGHT, wider, wider, bs, br)
        for i in LEVEL:

            @pl.when(source_of(i))
            def _():
                side_half(i, 0).wait_recv()
                side_half(i, 1).wait_recv()

    def rows_back(table, outs, spec, other, conj):
        back = []
        for g in (0, 1):
            unfold(g, outs[g], spec, other, conj)
            back.append(dot3(pair(table), pair(mixed, cols=groups[g][0])))
        return back

    def own_values(back):
        v = dot3(halves(back[0]), pair(own_inv))
        w = dot3(halves(back[1]), pair(own_inv1))
        vr, vi = v[:, :side], v[:, side:]
        return vr + w, 0.5 * vr - ROOT * vi - w

    fetch[2].wait()
    fetch[3].wait()
    own_columns(wide)

    full[block(row), :] = own[...]
    for k in range(1, pairs):
        gather(k).wait_recv()
        gather(k + pairs - 1).start()
    gather(0).wait_recv()
    for k in range(pairs, 2 * pairs - 1):
        gather(k).wait_recv()
    fetch[0].wait()
    fetch[7].wait()
    turned = halves(full[...])
    for g in (0, 1):
        lines = halves(dot3(turned, pair(lag_fwd, cols=groups[g][0])))
        unfold(g, rows_of(row_lag, lines, lines), spec_k, None, False)

    for k in (1, 4, 5, 6, 8, 9, 10):
        fetch[k].wait()
    loads[2].wait()
    receive(SIDES, wide, wide, hs, hr)
    outer_columns(wide)
    receive(CORNERS, wide, wide, hs, hr)
    outs = spectrum_of(wide)
    for g in (0, 1):
        unfold(g, outs[g], spec_i, spec_k, False)
    sums[...] = jnp.zeros_like(sums)
    for which in (0, 1):
        rows = half(which)
        x0, x1 = own_values(
            [dot3(pair(inv_own, rows), pair(mixed, cols=every)) for every, _, _ in groups]
        )
        x0, x1 = x0 - obs[rows, :side], x1 - obs[rows, side:]
        wider[rows, :side] = x0
        wider[rows, side:tile_cols] = x1
        send_half(which)
        sums[0:1] = sums[0:1] + line(x0) + line(x1)
    own_columns(wider)
    outs = []
    for every, _, _ in groups:
        lines = halves(near_t[:, every])
        outs.append(rows_of(row_own, lines, lines))
    for g in (0, 1):
        unfold(g, outs[g], None, spec_i, True)

    def lag_rows(rows):
        back = [dot3(pair(inv_lag, rows), pair(mixed, cols=every)) for every, _, _ in groups]
        return dot3(halves(jnp.concatenate(back, axis=1)), pair(lag_inv))

    def share(c):
        return pl.ds(pl.multiple_of(c * margin, margin), margin)

    kgrad[...] = lag_rows(share(1 - core))
    swap = copy(kgrad, pland, ps.at[0], ps.at[1], row=twin)
    swap.start()
    mine = lag_rows(share(core))
    swap.wait()
    mine = mine + pland[...]
    for k in range(pairs * n_col):
        cpart[k] = mine[k * few : (k + 1) * few]
    half_row = row // 2
    scatter = []
    for s, t in others(pairs, n_col):
        r, c = lax.rem(half_row + s, pairs), lax.rem(col + t, n_col)
        k = s * n_col + t - 1
        scatter.append(copy(
            cpart.at[r * n_col + c], cland.at[k], cs.at[k], cr.at[k], row=2 * r + core, col=c
        ))

    for k in range(2 * pairs - 1):
        gather(k).wait_send()
    for i in range(8):

        @pl.when(target_of(i))
        def _():
            halo(i, wide, wide, hs, hr).wait_send()

    receive_sides()
    for one in scatter:
        one.start()
    outer_columns(wider)
    receive(CORNERS, wider, wider, bs, br)
    x0, x1 = own_values(rows_back(inv_own, spectrum_of(wider), None, spec_k, True))
    refined[:, :side] = x0
    refined[:, side:] = x1
    sums[1:2] = line(x0) + line(x1)

    for i in range(8):

        @pl.when(target_of(i))
        def _():
            if i in LEVEL:
                side_half(i, 0).wait_send()
                side_half(i, 1).wait_send()
            else:
                halo(i, wider, wider, bs, br).wait_send()

    piece = cpart[half_row * n_col + col]
    for k, one in enumerate(scatter):
        one.wait()
        piece = piece + cland[k]
    pieces[col] = piece
    sums[2:3] = line(piece)
    gathers = [
        copy(pieces.at[col], pieces.at[col], gs.at[s - 1], gr.at[s - 1], col=lax.rem(col + s, n_col))
        for s in range(1, n_col)
    ]

    def total_of(buf):
        added = buf[0]
        for k in range(1, buf.shape[0]):
            added = added + buf[k]
        return added

    if n_row * n_col <= FEW:
        me = row * n_col + col
        srow[me] = sums[...]
        parts_ = [
            copy(srow.at[me], srow.at[me], as_.at[k], ar.at[k], **peer(row, col, s, t, n_row, n_col))
            for k, (s, t) in enumerate(others(n_row, n_col))
        ]
        for one in parts_ + gathers:
            one.start()
        for one in parts_:
            one.wait()
        added = total_of(srow)
    else:
        srow[row] = sums[...]
        parts_ = [
            copy(srow.at[row], srow.at[row], as_.at[s - 1], ar.at[s - 1], row=lax.rem(row + s, n_row))
            for s in range(1, n_row)
        ]
        for one in parts_ + gathers:
            one.start()
        for one in parts_:
            one.wait()
        scol[col] = total_of(srow)
        parts_ = [
            copy(scol.at[col], scol.at[col], es.at[s - 1], er.at[s - 1], col=lax.rem(col + s, n_col))
            for s in range(1, n_col)
        ]
        for one in parts_:
            one.start()
        for one in parts_:
            one.wait()
        added = total_of(scol)
    loss = 0.5 * jnp.sum(added[0:1], keepdims=True)
    image_norm = jnp.sum(added[1:2], keepdims=True)
    kernel_norm = jnp.sum(added[2:3], keepdims=True)
    refined[...] = wide[near, :tile_cols] - refined[...] * (loss / (image_norm + EPSILON))
    rate = 0.25 * loss / (kernel_norm + EPSILON)
    for one in gathers:
        one.wait()
    for c in range(n_col):
        rows = slice(c * few, (c + 1) * few)
        new_kernel[rows, :] = own[rows, :] - pieces[c] * rate


def leave(refined, new_kernel, refined_out, kernel_out, sem):
    moves = [
        pltpu.make_async_copy(refined, refined_out, sem.at[0]),
        pltpu.make_async_copy(new_kernel, kernel_out, sem.at[1]),
    ]
    for one in moves:
        one.start()
    for one in moves:
        one.wait()


def split(x):
    high = np.asarray(x, np.float32).astype(jnp.bfloat16)
    low = (np.asarray(x, np.float32) - high.astype(np.float32)).astype(jnp.bfloat16)
    return jnp.asarray(np.stack([high, low]))


def make_tables(n_row, owner, side):
    margin = side // 2
    wide, tall = 3 * side, 2 * side
    scale = 2.0 / (wide * tall) / side
    inside, centred = np.arange(side), np.arange(side) - margin

    def waves(places, freqs, period):
        phase = np.mod(np.outer(places, freqs), period) * (2 * math.pi / period)
        return np.cos(phase), np.sin(phase)

    first, second = 6 * np.arange(side) + 1, 6 * np.arange(margin) + 3

    def line_table(places):
        c0, s0 = waves(places, first, 2 * wide)
        c1, s1 = waves(places, second, 2 * wide)
        return np.concatenate([c0, -s0, c1, -s1], axis=1)

    c0, s0 = waves(inside, first, 2 * wide)
    c1, s1 = waves(inside, second, 2 * wide)
    own_fwd = np.block([[c0, -s0], [s0, c0]])
    own_fwd1 = np.concatenate([c1, -s1], axis=1)
    beside = np.concatenate([2 * side + np.arange(margin), np.arange(margin) - margin])

    def row_table(places):
        j = np.arange(margin)
        ce, se = waves(2 * j, places, tall)
        se[0] = np.cos(math.pi * places)
        co, so = waves(2 * j + 1, places, tall)
        return np.concatenate([ce, se, co, so], axis=0)

    blocks = list(range(0, n_row, 2)) + list(range(1, n_row, 2))
    turned = np.concatenate([np.arange(r * owner, (r + 1) * owner) for r in blocks])
    lag = line_table(centred)
    return [
        split(x)
        for x in (
            lag, lag.T * scale, own_fwd, own_fwd1, line_table(beside), own_fwd.T * scale,
            own_fwd1.T * scale, row_table(centred), row_table(inside), row_table(inside).T,
            row_table(centred).T[turned],
        )
    ]


def per_device(n_row, n_col, observed, estimate, kernel):
    tile_rows, tile_cols = observed.shape
    owner, side = kernel.shape
    margin = side // 2
    rows_long, cols_long = tile_rows + side, tile_cols + side
    tables = make_tables(n_row, owner, side)
    dma = pltpu.SemaphoreType.DMA
    more_c = max(n_col - 1, 1)
    few = owner // n_col
    pairs = n_row // 2
    firsts = n_row * n_col if n_row * n_col <= FEW else n_row
    spectrum = VMEM((rows_long, cols_long), F32)
    more_p = max(pairs * n_col - 1, 1)
    outs = pl.pallas_call(
        functools.partial(body, n_row, n_col),
        out_shape=(
            VMEM((tile_rows, tile_cols), F32),
            VMEM((owner, side), F32),
        ),
        in_specs=[pl.BlockSpec(memory_space=pl.ANY)] * (3 + len(tables)),
        out_specs=(pl.BlockSpec(memory_space=VMEM),) * 2,
        scratch_shapes=[VMEM(x.shape, BF16) for x in tables] + [
            spectrum,
            spectrum,
            VMEM((tile_rows, tile_cols), F32),
            VMEM((owner, side), F32),
            VMEM((side, side), F32),
            VMEM((tile_rows, cols_long), F32),
            VMEM((side, cols_long), F32),
            spectrum,
            spectrum,
            VMEM((2, rows_long, cols_long), BF16),
            VMEM((margin, side), F32),
            VMEM((margin, side), F32),
            VMEM((pairs * n_col, few, side), F32),
            VMEM((more_p, few, side), F32),
            VMEM((n_col, few, side), F32),
            VMEM((firsts, 8, 128), F32),
            VMEM((n_col, 8, 128), F32),
            VMEM((8, 128), F32),
            dma((3 + len(tables),)),
            dma((8,)), dma((8,)),
            dma((n_row,)), dma((n_row,)),
            dma((10,)), dma((10,)),
            dma((2,)),
            dma((more_p,)), dma((more_p,)),
            dma((more_c,)), dma((more_c,)),
            dma((firsts,)), dma((firsts,)),
            dma((more_c,)), dma((more_c,)),
        ],
        compiler_params=pltpu.CompilerParams(
            collective_id=0, has_side_effects=True, vmem_limit_bytes=56 * 1024 * 1024
        ),
        name="deconvolve",
    )(observed, estimate, kernel, *tables)
    return pl.pallas_call(
        leave,
        out_shape=tuple(jax.ShapeDtypeStruct(x.shape, F32) for x in (observed, kernel)),
        in_specs=[pl.BlockSpec(memory_space=VMEM)] * 2,
        out_specs=(pl.BlockSpec(memory_space=pl.ANY),) * 2,
        scratch_shapes=[dma((2,))],
        name="leave",
    )(*[pltpu.with_memory_space_constraint(x, VMEM) for x in outs])


def solution(mesh):
    placed = (P(("groups", "row"), "col"), P(("groups", "row"), "col"), P(("groups", "row"), None))
    return jax.shard_map(
        functools.partial(per_device, mesh.shape["row"], mesh.shape["col"]),
        mesh=mesh,
        in_specs=placed,
        out_specs=(P(("groups", "row"), "col"), P(("groups", "row"), None)),
        check_vma=False,
    )
```

```python
import functools
import math

import jax
import jax.numpy as jnp
import numpy as np
from jax import lax
from jax.experimental import pallas as pl
from jax.experimental.pallas import tpu as pltpu
from jax.sharding import PartitionSpec as P

EPSILON = 1e-06
MESH = pl.DeviceIdType.MESH
FEW = 16
VMEM = pltpu.VMEM
BF16 = jnp.bfloat16
F32 = jnp.float32
ROOT = math.sqrt(3.0) / 2.0
AROUND = [(a, b) for a in (-1, 0, 1) for b in (-1, 0, 1) if (a, b) != (0, 0)]
SIDES = [i for i, (a, b) in enumerate(AROUND) if a * b == 0]
LEVEL = [i for i, (a, b) in enumerate(AROUND) if a == 0]
UPRIGHT = [i for i, (a, b) in enumerate(AROUND) if b == 0]
CORNERS = [i for i, (a, b) in enumerate(AROUND) if a * b != 0]


def here(row, col, n_row, n_col):
    return (row >= 0) & (row < n_row) & (col >= 0) & (col < n_col)


def others(n_row, n_col):
    return [(s, t) for s in range(n_row) for t in range(n_col) if (s, t) != (0, 0)]


def peer(row, col, s, t, n_row, n_col):
    return {"row": lax.rem(row + s, n_row), "col": lax.rem(col + t, n_col)}


def spans(tile, margin):
    inner = {-1: (0, margin), 0: (0, tile), 1: (tile - margin, margin)}
    outer = {-1: (tile + margin, margin), 0: (0, tile), 1: (tile, margin)}
    return inner, outer


def at(ref, rows, cols):
    return ref.at[pl.ds(*rows), pl.ds(*cols)]


def line(x):
    rows, cols = x.shape
    if rows % 8:
        x = jnp.concatenate([x, jnp.zeros((8 - rows % 8, cols), F32)], axis=0)
        rows = x.shape[0]
    x = (x * x).reshape(rows // 8, 8, cols).sum(axis=0)
    total = x[:, :128]
    for at_col in range(128, cols, 128):
        total = total + x[:, at_col : at_col + 128]
    return jnp.sum(total, axis=0, keepdims=True)


def halves(x):
    high = x.astype(BF16)
    return high, (x - high.astype(F32)).astype(BF16)


def dot3(a, b):
    dot = lambda p, q: lax.dot_general(p, q, (((1,), (0,)), ((), ())), preferred_element_type=F32)
    return dot(a[0], b[0]) + (dot(a[0], b[1]) + dot(a[1], b[0]))


def body(
    n_row, n_col, observed, estimate, kernel, *rest
):
    tables, rest = rest[:11], rest[11:]
    refined, new_kernel = rest[:2]
    held, rest = rest[2:13], rest[13:]
    (wide, wider, obs, own, full, near_t, far_t, spec_i, spec_k, mixed, kgrad, pland,
     cpart, cland, pieces, srow, scol, sums, *sems) = rest
    (ls, hs, hr, ks, kr, bs, br, ps, cs, cr, gs, gr, as_, ar, es, er) = sems
    (lag_fwd, lag_inv, own_fwd, own_fwd1, side_fwd, own_inv, own_inv1,
     row_lag, row_own, inv_own, inv_lag) = held
    row, col = lax.axis_index("row"), lax.axis_index("col")
    tile_rows, tile_cols = observed.shape
    owner, side = kernel.shape
    margin = side // 2
    rows_long, cols_long = tile_rows + side, tile_cols + side
    in_r, out_r = spans(tile_rows, margin)
    in_c, out_c = spans(tile_cols, margin)
    pairs = n_row // 2
    core = lax.rem(row, 2)
    twin = row + 1 - 2 * core
    few = owner // n_col

    def copy(src, dst, ssem, rsem, **target):
        return pltpu.make_async_remote_copy(
            src_ref=src, dst_ref=dst, send_sem=ssem, recv_sem=rsem,
            device_id=target, device_id_type=MESH,
        )

    def halo(i, src, dst, ssem, rsem):
        dr, dc = AROUND[i]
        return copy(
            at(src, in_r[dr], in_c[dc]), at(dst, out_r[-dr], out_c[-dc]),
            ssem.at[i], rsem.at[i], row=row + dr, col=col + dc,
        )

    def target_of(i):
        dr, dc = AROUND[i]
        return here(row + dr, col + dc, n_row, n_col)

    def source_of(i):
        dr, dc = AROUND[i]
        return here(row - dr, col - dc, n_row, n_col)

    def block(r):
        return pl.ds(pl.multiple_of(r * owner, owner), owner)

    barrier = pltpu.get_barrier_semaphore()
    for s, t in sorted(others(n_row, n_col), key=lambda o: min(o[0], n_row - o[0]) + min(o[1], n_col - o[1])):
        pl.semaphore_signal(
            barrier, inc=1, device_id=peer(row, col, s, t, n_row, n_col), device_id_type=MESH
        )
    near, far = slice(0, tile_rows), slice(tile_rows, rows_long)
    loads = [
        pltpu.make_async_copy(estimate, wide.at[near, :tile_cols], ls.at[0]),
        pltpu.make_async_copy(kernel, own, ls.at[1]),
        pltpu.make_async_copy(observed, obs, ls.at[2]),
    ]
    order = (2, 3, 0, 7, 4, 8, 9, 5, 6, 10, 1)
    fetch = {
        k: pltpu.make_async_copy(tables[k], held[k], ls.at[3 + k]) for k in order
    }
    for one in loads[:2]:
        one.start()
    pl.semaphore_wait(barrier, n_row * n_col - 1)
    for one in loads[:2]:
        one.wait()

    def gather(k):
        if k == 0:
            return copy(own, full.at[block(row), :], ks.at[0], kr.at[0], row=twin)
        if k < pairs:
            there = lax.rem(row + 2 * k, n_row)
            return copy(own, full.at[block(row), :], ks.at[k], kr.at[k], row=there)
        behind = lax.rem(row + n_row - 2 * (k - pairs + 1), n_row)
        return copy(
            full.at[block(behind), :], full.at[block(behind), :], ks.at[k], kr.at[k], row=twin
        )

    def send(src, dst, ssem, rsem):
        for i in LEVEL + UPRIGHT + CORNERS:

            @pl.when(target_of(i))
            def _():
                halo(i, src, dst, ssem, rsem).start()

    def receive(some, src, dst, ssem, rsem):
        for i in some:

            @pl.when(source_of(i))
            def _():
                halo(i, src, dst, ssem, rsem).wait_recv()

    for k in range(pairs):
        gather(k).start()
    send(wide, wide, hs, hr)
    loads[2].start()
    for k in order:
        fetch[k].start()

    for i, (dr, dc) in enumerate(AROUND):

        @pl.when(jnp.logical_not(source_of(i)))
        def _():
            empty = jnp.zeros((out_r[-dr][1], out_c[-dc][1]), F32)
            wide[pl.ds(*out_r[-dr]), pl.ds(*out_c[-dc])] = empty
            wider[pl.ds(*out_r[-dr]), pl.ds(*out_c[-dc])] = empty

    def pair(ref, rows=slice(None), cols=slice(None)):
        return ref[0, rows, cols], ref[1, rows, cols]

    def three(x):
        return x[:, :side], x[:, side : 2 * side]

    groups = (
        (slice(0, 2 * side), slice(0, side), slice(side, 2 * side)),
        (slice(2 * side, 3 * side), slice(2 * side, 2 * side + margin), slice(2 * side + margin, 3 * side)),
    )

    def columns(x0, x1):
        u, v, w = x0 + 0.5 * x1, -ROOT * x1, x0 - x1
        return (
            dot3(halves(jnp.concatenate([u, v], axis=1)), pair(own_fwd)),
            dot3(halves(w), pair(own_fwd1)),
        )

    def rows_of(table, even, odd):
        return (
            dot3(pair(table, slice(0, side)), even),
            dot3(pair(table, slice(side, 2 * side)), odd),
        )

    def unfold(g, outs, spec, other, conj):
        step = 16
        every, re, im = groups[g]
        half = re.stop - re.start
        for base, out in zip((0, side), outs):
            for k in range(margin // step):
                here_ = slice(k * step, (k + 1) * step)
                there = slice(margin + k * step, margin + (k + 1) * step)
                up = slice(base + k * step, base + (k + 1) * step)
                down = slice(base + margin + k * step, base + margin + (k + 1) * step)
                first = None
                if base == 0 and k == 0:
                    first = lax.broadcasted_iota(jnp.int32, (step, half), 0) == 0
                pr, pi, qr, qi = out[here_, :half], out[here_, half:], out[there, :half], out[there, half:]
                ur, ui, dr, di = pr + qi, pi - qr, pr - qi, pi + qr
                if first is not None:
                    ur, ui = jnp.where(first, pr, ur), jnp.where(first, pi, ui)
                    dr, di = jnp.where(first, qr, dr), jnp.where(first, qi, di)
                if spec is not None:
                    spec[up, re], spec[up, im] = ur, ui
                    spec[down, re], spec[down, im] = dr, di
                if other is None:
                    continue
                both = []
                for rows, xr, xi in ((up, ur, ui), (down, dr, di)):
                    yr, yi = other[rows, re], other[rows, im]
                    if conj:
                        both.append((xr * yr + xi * yi, xi * yr - xr * yi))
                    else:
                        both.append((xr * yr - xi * yi, xr * yi + xi * yr))
                (ur, ui), (dr, di) = both
                cr_, ci_, sr_, si_ = ur + dr, ui + di, di - ui, ur - dr
                if first is not None:
                    cr_, ci_ = jnp.where(first, ur, cr_), jnp.where(first, ui, ci_)
                    sr_, si_ = jnp.where(first, dr, sr_), jnp.where(first, di, si_)
                for rows, cols, v in ((up, re, cr_), (up, im, ci_), (down, re, sr_), (down, im, si_)):
                    high, low = halves(v)
                    mixed[0, rows, cols] = high
                    mixed[1, rows, cols] = low

    def own_columns(ref):
        for (every, _, _), part in zip(groups, columns(*three(ref[near, :tile_cols]))):
            near_t[:, every] = part

    def outer_columns(ref):
        aside = halves(ref[near, tile_cols:])
        below = columns(*three(ref[far, :tile_cols]))
        for (every, _, _), part in zip(groups, below):
            near_t[:, every] = near_t[:, every] + dot3(aside, pair(side_fwd, cols=every))
            far_t[:, every] = part

    def spectrum_of(ref):
        corner = halves(ref[far, tile_cols:])
        outs = []
        for every, _, _ in groups:
            beside = near_t[:, every]
            below = far_t[:, every] + dot3(corner, pair(side_fwd, cols=every))
            outs.append(rows_of(row_own, halves(beside + below), halves(beside - below)))
        return outs

    def half(which):
        return pl.ds(pl.multiple_of(margin * (which + core - 2 * which * core), margin), margin)

    def side_half(i, which):
        dc = AROUND[i][1]
        k = i + 5 * which
        return copy(
            wider.at[half(which), pl.ds(*in_c[dc])], wider.at[half(which), pl.ds(*out_c[-dc])],
            bs.at[k], br.at[k], row=row, col=col + dc,
        )

    def outward(i):
        dr = AROUND[i][0]
        return core == (1 if dr == 1 else 0)

    def send_half(which):
        for i in UPRIGHT + LEVEL + CORNERS:
            level = i in LEVEL
            there = target_of(i)
            if not level:
                there = there & (outward(i) if which == 0 else jnp.logical_not(outward(i)))

            @pl.when(there)
            def _():
                (side_half(i, which) if level else halo(i, wider, wider, bs, br)).start()

    def receive_sides():
        receive(UPRIGHT, wider, wider, bs, br)
        for i in LEVEL:

            @pl.when(source_of(i))
            def _():
                side_half(i, 0).wait_recv()
                side_half(i, 1).wait_recv()

    def rows_back(table, outs, spec, other, conj):
        back = []
        for g in (0, 1):
            unfold(g, outs[g], spec, other, conj)
            back.append(dot3(pair(table), pair(mixed, cols=groups[g][0])))
        return back

    def own_values(back):
        v = dot3(halves(back[0]), pair(own_inv))
        w = dot3(halves(back[1]), pair(own_inv1))
        vr, vi = v[:, :side], v[:, side:]
        return vr + w, 0.5 * vr - ROOT * vi - w

    fetch[2].wait()
    fetch[3].wait()
    own_columns(wide)

    full[block(row), :] = own[...]
    for k in range(1, pairs):
        gather(k).wait_recv()
        gather(k + pairs - 1).start()
    gather(0).wait_recv()
    for k in range(pairs, 2 * pairs - 1):
        gather(k).wait_recv()
    fetch[0].wait()
    fetch[7].wait()
    turned = halves(full[...])
    for g in (0, 1):
        lines = halves(dot3(turned, pair(lag_fwd, cols=groups[g][0])))
        unfold(g, rows_of(row_lag, lines, lines), spec_k, None, False)

    for k in (1, 4, 5, 6, 8, 9, 10):
        fetch[k].wait()
    loads[2].wait()
    receive(SIDES, wide, wide, hs, hr)
    outer_columns(wide)
    receive(CORNERS, wide, wide, hs, hr)
    outs = spectrum_of(wide)
    for g in (0, 1):
        unfold(g, outs[g], spec_i, spec_k, False)
    sums[...] = jnp.zeros_like(sums)
    for which in (0, 1):
        rows = half(which)
        x0, x1 = own_values(
            [dot3(pair(inv_own, rows), pair(mixed, cols=every)) for every, _, _ in groups]
        )
        x0, x1 = x0 - obs[rows, :side], x1 - obs[rows, side:]
        wider[rows, :side] = x0
        wider[rows, side:tile_cols] = x1
        send_half(which)
        sums[0:1] = sums[0:1] + line(x0) + line(x1)
    own_columns(wider)
    outs = []
    for every, _, _ in groups:
        lines = halves(near_t[:, every])
        outs.append(rows_of(row_own, lines, lines))
    for g in (0, 1):
        unfold(g, outs[g], None, spec_i, True)

    def lag_rows(rows):
        back = [dot3(pair(inv_lag, rows), pair(mixed, cols=every)) for every, _, _ in groups]
        return dot3(halves(jnp.concatenate(back, axis=1)), pair(lag_inv))

    def share(c):
        return pl.ds(pl.multiple_of(c * margin, margin), margin)

    kgrad[...] = lag_rows(share(1 - core))
    swap = copy(kgrad, pland, ps.at[0], ps.at[1], row=twin)
    swap.start()
    mine = lag_rows(share(core))
    swap.wait()
    mine = mine + pland[...]
    for k in range(pairs * n_col):
        cpart[k] = mine[k * few : (k + 1) * few]
    half_row = row // 2
    scatter = []
    for s, t in others(pairs, n_col):
        r, c = lax.rem(half_row + s, pairs), lax.rem(col + t, n_col)
        k = s * n_col + t - 1
        scatter.append(copy(
            cpart.at[r * n_col + c], cland.at[k], cs.at[k], cr.at[k], row=2 * r + core, col=c
        ))

    for k in range(2 * pairs - 1):
        gather(k).wait_send()
    for i in range(8):

        @pl.when(target_of(i))
        def _():
            halo(i, wide, wide, hs, hr).wait_send()

    receive_sides()
    for one in scatter:
        one.start()
    outer_columns(wider)
    receive(CORNERS, wider, wider, bs, br)
    x0, x1 = own_values(rows_back(inv_own, spectrum_of(wider), None, spec_k, True))
    refined[:, :side] = x0
    refined[:, side:] = x1
    sums[1:2] = line(x0) + line(x1)

    for i in range(8):

        @pl.when(target_of(i))
        def _():
            if i in LEVEL:
                side_half(i, 0).wait_send()
                side_half(i, 1).wait_send()
            else:
                halo(i, wider, wider, bs, br).wait_send()

    piece = cpart[half_row * n_col + col]
    for k, one in enumerate(scatter):
        one.wait()
        piece = piece + cland[k]
    pieces[col] = piece
    sums[2:3] = line(piece)
    gathers = [
        copy(pieces.at[col], pieces.at[col], gs.at[s - 1], gr.at[s - 1], col=lax.rem(col + s, n_col))
        for s in range(1, n_col)
    ]

    def total_of(buf):
        added = buf[0]
        for k in range(1, buf.shape[0]):
            added = added + buf[k]
        return added

    if n_row * n_col <= FEW:
        me = row * n_col + col
        srow[me] = sums[...]
        parts_ = [
            copy(srow.at[me], srow.at[me], as_.at[k], ar.at[k], **peer(row, col, s, t, n_row, n_col))
            for k, (s, t) in enumerate(others(n_row, n_col))
        ]
        for one in parts_ + gathers:
            one.start()
        for one in parts_:
            one.wait()
        added = total_of(srow)
    else:
        srow[row] = sums[...]
        parts_ = [
            copy(srow.at[row], srow.at[row], as_.at[s - 1], ar.at[s - 1], row=lax.rem(row + s, n_row))
            for s in range(1, n_row)
        ]
        for one in parts_ + gathers:
            one.start()
        for one in parts_:
            one.wait()
        scol[col] = total_of(srow)
        parts_ = [
            copy(scol.at[col], scol.at[col], es.at[s - 1], er.at[s - 1], col=lax.rem(col + s, n_col))
            for s in range(1, n_col)
        ]
        for one in parts_:
            one.start()
        for one in parts_:
            one.wait()
        added = total_of(scol)
    loss = 0.5 * jnp.sum(added[0:1], keepdims=True)
    image_norm = jnp.sum(added[1:2], keepdims=True)
    kernel_norm = jnp.sum(added[2:3], keepdims=True)
    refined[...] = wide[near, :tile_cols] - refined[...] * (loss / (image_norm + EPSILON))
    rate = 0.25 * loss / (kernel_norm + EPSILON)
    for one in gathers:
        one.wait()
    for c in range(n_col):
        rows = slice(c * few, (c + 1) * few)
        new_kernel[rows, :] = own[rows, :] - pieces[c] * rate


def leave(refined, new_kernel, refined_out, kernel_out, sem):
    moves = [
        pltpu.make_async_copy(refined, refined_out, sem.at[0]),
        pltpu.make_async_copy(new_kernel, kernel_out, sem.at[1]),
    ]
    for one in moves:
        one.start()
    for one in moves:
        one.wait()


def split(x):
    high = np.asarray(x, np.float32).astype(jnp.bfloat16)
    low = (np.asarray(x, np.float32) - high.astype(np.float32)).astype(jnp.bfloat16)
    return jnp.asarray(np.stack([high, low]))


def make_tables(n_row, owner, side):
    margin = side // 2
    wide, tall = 3 * side, 2 * side
    scale = 2.0 / (wide * tall) / side
    inside, centred = np.arange(side), np.arange(side) - margin

    def waves(places, freqs, period):
        phase = np.mod(np.outer(places, freqs), period) * (2 * math.pi / period)
        return np.cos(phase), np.sin(phase)

    first, second = 6 * np.arange(side) + 1, 6 * np.arange(margin) + 3

    def line_table(places):
        c0, s0 = waves(places, first, 2 * wide)
        c1, s1 = waves(places, second, 2 * wide)
        return np.concatenate([c0, -s0, c1, -s1], axis=1)

    c0, s0 = waves(inside, first, 2 * wide)
    c1, s1 = waves(inside, second, 2 * wide)
    own_fwd = np.block([[c0, -s0], [s0, c0]])
    own_fwd1 = np.concatenate([c1, -s1], axis=1)
    beside = np.concatenate([2 * side + np.arange(margin), np.arange(margin) - margin])

    def row_table(places):
        j = np.arange(margin)
        ce, se = waves(2 * j, places, tall)
        se[0] = np.cos(math.pi * places)
        co, so = waves(2 * j + 1, places, tall)
        return np.concatenate([ce, se, co, so], axis=0)

    blocks = list(range(0, n_row, 2)) + list(range(1, n_row, 2))
    turned = np.concatenate([np.arange(r * owner, (r + 1) * owner) for r in blocks])
    lag = line_table(centred)
    return [
        split(x)
        for x in (
            lag, lag.T * scale, own_fwd, own_fwd1, line_table(beside), own_fwd.T * scale,
            own_fwd1.T * scale, row_table(centred), row_table(inside), row_table(inside).T,
            row_table(centred).T[turned],
        )
    ]


def per_device(n_row, n_col, observed, estimate, kernel):
    tile_rows, tile_cols = observed.shape
    owner, side = kernel.shape
    margin = side // 2
    rows_long, cols_long = tile_rows + side, tile_cols + side
    tables = make_tables(n_row, owner, side)
    dma = pltpu.SemaphoreType.DMA
    more_c = max(n_col - 1, 1)
    few = owner // n_col
    pairs = n_row // 2
    firsts = n_row * n_col if n_row * n_col <= FEW else n_row
    spectrum = VMEM((rows_long, cols_long), F32)
    more_p = max(pairs * n_col - 1, 1)
    outs = pl.pallas_call(
        functools.partial(body, n_row, n_col),
        out_shape=(
            VMEM((tile_rows, tile_cols), F32),
            VMEM((owner, side), F32),
        ),
        in_specs=[pl.BlockSpec(memory_space=pl.ANY)] * (3 + len(tables)),
        out_specs=(pl.BlockSpec(memory_space=VMEM),) * 2,
        scratch_shapes=[VMEM(x.shape, BF16) for x in tables] + [
            spectrum,
            spectrum,
            VMEM((tile_rows, tile_cols), F32),
            VMEM((owner, side), F32),
            VMEM((side, side), F32),
            VMEM((tile_rows, cols_long), F32),
            VMEM((side, cols_long), F32),
            spectrum,
            spectrum,
            VMEM((2, rows_long, cols_long), BF16),
            VMEM((margin, side), F32),
            VMEM((margin, side), F32),
            VMEM((pairs * n_col, few, side), F32),
            VMEM((more_p, few, side), F32),
            VMEM((n_col, few, side), F32),
            VMEM((firsts, 8, 128), F32),
            VMEM((n_col, 8, 128), F32),
            VMEM((8, 128), F32),
            dma((3 + len(tables),)),
            dma((8,)), dma((8,)),
            dma((n_row,)), dma((n_row,)),
            dma((10,)), dma((10,)),
            dma((2,)),
            dma((more_p,)), dma((more_p,)),
            dma((more_c,)), dma((more_c,)),
            dma((firsts,)), dma((firsts,)),
            dma((more_c,)), dma((more_c,)),
        ],
        compiler_params=pltpu.CompilerParams(
            collective_id=0, has_side_effects=True, vmem_limit_bytes=56 * 1024 * 1024
        ),
        name="deconvolve",
    )(observed, estimate, kernel, *tables)
    return pl.pallas_call(
        leave,
        out_shape=tuple(jax.ShapeDtypeStruct(x.shape, F32) for x in (observed, kernel)),
        in_specs=[pl.BlockSpec(memory_space=VMEM)] * 2,
        out_specs=(pl.BlockSpec(memory_space=pl.ANY),) * 2,
        scratch_shapes=[dma((2,))],
        name="leave",
    )(*[pltpu.with_memory_space_constraint(x, VMEM) for x in outs])


def solution(mesh):
    placed = (P(("groups", "row"), "col"), P(("groups", "row"), "col"), P(("groups", "row"), None))
    return jax.shard_map(
        functools.partial(per_device, mesh.shape["row"], mesh.shape["col"]),
        mesh=mesh,
        in_specs=placed,
        out_specs=(P(("groups", "row"), "col"), P(("groups", "row"), None)),
        check_vma=False,
    )
```
